256 devices in a mesh: row: 16 (over x_lo, z), col: 16 (over x_hi, y, core).
Axes of the slice: x: 4 (x_hi: 2, x_lo: 2; x = x_hi * 2 + x_lo), y: 4, z: 8, core: 2. Of those that a mesh axis runs over, the one named last changes fastest.
Arguments:
- adjoints: bfloat16 [4096, 16, 200], P(('row', 'col')), may hold values from -6 to 6
- jac_blocks: bfloat16 [16, 16, 128, 200, 200], P('row', 'col'), may hold values from -0.4375 to 0.4375
- jac_rows: int32 [16, 16, 128], P('row', 'col'), may hold values from 0 to 255, as said below
- jac_cols: int32 [16, 16, 128], P('row', 'col'), may hold values from 0 to 255, as said below
- tile_count: int32 [16, 16], P('row', 'col'), may hold values from 32 to 128, as said below
Outputs:
- transposed: bfloat16 [4096, 16, 200], P('col')
The draws below stay inside these ranges and needn't reach their ends.
Inputs may be any that keep to these rules, and one draw needn't show every extreme that they name: `jac_rows`: row faces within a tile; both ends are named by some slot. `jac_cols`: column faces within a tile; both ends are named by some slot. `tile_count`: slots at or above the count are padding and are ignored; some tile has exactly 128 live slots.
All inputs are finite; a program needn't handle non-finite values.
Results may differ from the reference program's by a relative error of at most 0.001.
Values may be sent and summed in bfloat16 or wider, within the bound.
No kernel may reach another device: no remote copies, remote signals or barrier semaphores. Data moves between devices by JAX's collectives and lax.ppermute only.
A program may use at most 64 MiB of HBM per device.

```python
import jax
import jax.numpy as jnp
from jax import lax

B = 200
K = 16
NB = 4096
BROW = 256
BCOL = 256
CAP = 128
N_ROW = 16
N_COL = 16


def draw_jac_rows(key, part):
    row_index = jax.random.randint(jax.random.fold_in(key, 11), (N_ROW, N_COL, CAP), 0, BROW)
    row_index = row_index.at[0, 0, 0].set(BROW - 1).at[0, 0, 1].set(0)
    return row_index.astype(jnp.int32)


def draw_jac_cols(key, part):
    col_index = jax.random.randint(jax.random.fold_in(key, 23), (N_ROW, N_COL, CAP), 0, BCOL)
    col_index = col_index.at[0, 0, 0].set(0).at[0, 0, 1].set(BCOL - 1)
    return col_index.astype(jnp.int32)


def draw_tile_count(key, part):
    counts = jax.random.randint(jax.random.fold_in(key, 31), (N_ROW * N_COL,), CAP // 4, 3 * CAP // 4 + 1)
    chosen = jax.random.randint(jax.random.fold_in(key, 37), (), 0, N_ROW * N_COL)
    flattened = counts.at[chosen].set(CAP)
    return flattened.reshape((N_ROW, N_COL)).astype(jnp.int32)


def steps_of(own_key, shape, pieces, least, top_value):
    gain = 1.0
    for dim, shards_of in pieces:
        heights = jax.random.uniform(jax.random.fold_in(jax.random.fold_in(own_key, 6), dim), (shards_of,), jnp.float32, least / len(pieces), top_value / len(pieces))
        gain = gain * jnp.repeat(jnp.exp(heights), shape[dim] // shards_of).reshape((-1,) + (1,) * (len(shape) - 1 - dim))
    return gain


def normal_values(own_key, extent, deviation, limit, shards=(), kind=jnp.bfloat16):
    result = deviation * jax.random.normal(own_key, extent, jnp.float32)
    if shards:
        result = result * steps_of(own_key, extent, shards, -0.22, 0.18)
    return jnp.clip(result, -limit, limit).astype(kind)


def setup_inputs(seed: int = 0) -> dict:
    key_list = jax.random.split(jax.random.key(seed), 6)
    return {
        "adjoints": normal_values(key_list[0], (NB, K, B), 1.0, 6.0, ((0, 256),)),
        "jac_blocks": normal_values(key_list[1], (N_ROW, N_COL, CAP, B, B), B ** -0.5, 0.4375, ((0, 16), (1, 16))),
        "jac_rows": draw_jac_rows(jax.random.fold_in(key_list[5], 71), 0),
        "jac_cols": draw_jac_cols(jax.random.fold_in(key_list[5], 71), 0),
        "tile_count": draw_tile_count(jax.random.fold_in(key_list[5], 71), 0),
    }


def reference(adjoints, jac_blocks, jac_rows, jac_cols, tile_count):
    accumulated = jnp.zeros((NB, K, B), jnp.float32)

    def one_tile(running, tile_index):
        row_tile = tile_index // N_COL
        col_tile = tile_index % N_COL
        blocks = jac_blocks[row_tile, col_tile].astype(jnp.float32)
        face_rows = (row_tile * BROW + jac_rows[row_tile, col_tile]).astype(jnp.int32)
        picked = jnp.take(adjoints, face_rows, axis=0).astype(jnp.float32)
        products = jnp.einsum("skd,sde->ske", picked, blocks)
        live_slot = jnp.arange(CAP, dtype=jnp.int32) < tile_count[row_tile, col_tile]
        face_cols = jnp.where(live_slot, col_tile * BCOL + jac_cols[row_tile, col_tile], NB).astype(jnp.int32)
        running = running.at[face_cols].add(products, mode="drop")
        return running, None

    accumulated, _ = lax.scan(one_tile, accumulated, jnp.arange(N_ROW * N_COL, dtype=jnp.int32))
    return accumulated.astype(jnp.bfloat16)
```

```python
import functools

import jax
import jax.numpy as jnp
from jax import lax
from jax.experimental import pallas as pl
from jax.experimental.pallas import tpu as pltpu
from jax.sharding import Mesh, PartitionSpec as P

AXES = ("xlo", "z", "xhi", "y", "core")
SIZES = (2, 8, 2, 4, 2)
ROW = ("xlo", "z")
COL = ("xhi", "y", "core")

BITS = 15
LIMIT = 32767.0
TINY = 1e-30


def pow2(exponent):
    return jnp.exp2(exponent).astype(jnp.bfloat16).astype(jnp.float32)


def terms_kernel(where_ref, own_ref, other_ref, jac_ref, cols_ref, out_ref, terms_ref, *, per_step, k, b, rows):
    step = pl.program_id(0)
    half = own_ref.shape[0]
    for j in range(per_step):
        slot = step * per_step + j
        place = where_ref[slot]
        inner = lax.rem(place, half)
        mine = own_ref[inner]
        theirs = other_ref[inner]
        lhs = jnp.where(place < half, mine, theirs)
        term = jnp.dot(lhs, jac_ref[j], preferred_element_type=jnp.float32)
        at = pl.ds(pl.multiple_of(slot * k, k), k)
        terms_ref[0, at, :] = term[:, :128]
        terms_ref[1, at, pl.ds(0, b - 128)] = term[:, 128:]

    @pl.when(step == pl.num_programs(0) - 1)
    def _():
        slots = cols_ref.shape[1]
        meta_row = lax.broadcasted_iota(jnp.int32, (8, slots), 0)
        cols = cols_ref[...].astype(jnp.float32)
        for i in range(k):
            at = pl.ds(i, slots, stride=k)
            left = jnp.transpose(terms_ref[0, at, :])
            right = jnp.transpose(terms_ref[1, at, :])[:b - 128]
            flipped = jnp.concatenate([left, right], axis=0)
            top = jnp.max(jnp.abs(flipped), axis=0, keepdims=True)
            exponent = jnp.ceil(jnp.log2(jnp.maximum(top, TINY)) + 0.01) - BITS
            scaled = jnp.clip(jnp.round(flipped * pow2(-exponent)), -LIMIT, LIMIT)
            meta = jnp.where(meta_row == 0, exponent, jnp.where(meta_row == 1, cols, 0.0))
            both = jnp.concatenate([scaled, meta], axis=0)
            out_ref[i] = both.astype(jnp.int32).astype(jnp.int16)


def make_terms(where, own, other, jac, cols):
    slots, b, _ = jac.shape
    faces, k, _ = own.shape
    per_step = 16
    rows = b + 8
    return pl.pallas_call(
        functools.partial(terms_kernel, per_step=per_step, k=k, b=b, rows=rows),
        out_shape=jax.ShapeDtypeStruct((k, rows, slots), jnp.int16),
        grid_spec=pltpu.PrefetchScalarGridSpec(
            num_scalar_prefetch=1,
            grid=(slots // per_step,),
            in_specs=[
                pl.BlockSpec((faces, k, b), lambda i, w: (0, 0, 0)),
                pl.BlockSpec((faces, k, b), lambda i, w: (0, 0, 0)),
                pl.BlockSpec((per_step, b, b), lambda i, w: (i, 0, 0)),
                pl.BlockSpec((1, slots), lambda i, w: (0, 0)),
            ],
            out_specs=pl.BlockSpec((k, rows, slots), lambda i, w: (0, 0, 0)),
            scratch_shapes=[pltpu.VMEM((2, slots * k, 128), jnp.float32)],
        ),
        name="terms",
    )(where, own, other, jac, cols)


def sum_kernel(got_ref, out_ref, lhs_ref, pick_ref):
    tiles, rows, slots = got_ref.shape
    b, faces = out_ref.shape
    face = lax.broadcasted_iota(jnp.int32, (faces, slots), 0)
    for t in range(tiles):
        got = got_ref[t].astype(jnp.int32)
        high = got[:b] >> 8
        low = got[:b] & 255
        scale = pow2(got[b:b + 1].astype(jnp.float32))
        cols = got[b + 1:b + 2]
        pick = jnp.where(face == cols, scale, 0.0)
        at = pl.ds(t * slots, slots)
        pick_ref[:, at] = pick.astype(jnp.bfloat16)
        lhs_ref[0:b, at] = (high.astype(jnp.float32) * 256.0).astype(jnp.bfloat16)
        lhs_ref[b:2 * b, at] = low.astype(jnp.float32).astype(jnp.bfloat16)
    both = lax.dot_general(
        lhs_ref[...], pick_ref[...], (((1,), (1,)), ((), ())), preferred_element_type=jnp.float32
    )
    out_ref[...] = (both[:b] + both[b:]).astype(jnp.bfloat16)


def add_up(got, faces):
    tiles, rows, slots = got.shape
    b = rows - 8
    return pl.pallas_call(
        sum_kernel,
        out_shape=jax.ShapeDtypeStruct((b, faces), jnp.bfloat16),
        scratch_shapes=[
            pltpu.VMEM((2 * b, tiles * slots), jnp.bfloat16),
            pltpu.VMEM((faces, tiles * slots), jnp.bfloat16),
        ],
        name="add_up",
    )(got)


def gather_result(mine):
    xlo = lax.axis_index("xlo")
    z = lax.axis_index("z")
    other = lax.ppermute(mine, "xlo", [(0, 1), (1, 0)])
    first = jnp.where(xlo == 0, mine, other)
    second = jnp.where(xlo == 0, other, mine)
    pair = jnp.stack([first, second])
    up = [(i, (i + 1) % 8) for i in range(8)]
    down = [(i, (i - 1) % 8) for i in range(8)]
    out = jnp.zeros((2, 8) + mine.shape, mine.dtype)

    def put(out, piece, at, x=0):
        return lax.dynamic_update_slice(out, piece[:, None], (x, lax.rem(at + 16, 8), 0, 0))

    below = above = pair
    pieces = [(pair, z, 0)]
    for d in range(1, 4):
        below = lax.ppermute(below, "z", up)
        above = lax.ppermute(above, "z", down)
        pieces += [(below, z - d, 0), (above, z + d, 0)]
    pieces.append((lax.ppermute(below[:1], "z", up), z - 4, 0))
    pieces.append((lax.ppermute(above[1:], "z", down), z + 4, 1))
    for piece, at, x in pieces:
        out = put(out, piece, at, x)
    return out


def on_device(adjoints, jac_blocks, jac_rows, jac_cols, tile_count):
    faces_here, k, b = adjoints.shape
    slots = jac_rows.shape[2]
    faces = faces_here * 16
    core = lax.axis_index("core")
    own = lax.all_to_all(jnp.broadcast_to(adjoints, (8,) + adjoints.shape), ("xhi", "y"), 0, 0)
    other = lax.ppermute(own, "core", [(0, 1), (1, 0)])
    own = own.reshape(faces // 2, k, b)
    other = other.reshape(faces // 2, k, b)
    slot_rows = jac_rows[0, 0]
    home = slot_rows // faces_here
    where = ((home % 2) ^ core) * (faces // 2) + (home // 2) * faces_here + slot_rows % faces_here
    live = jnp.arange(slots, dtype=jnp.int32) < tile_count[0, 0]
    cols = jnp.where(live, jac_cols[0, 0], -1)[None]
    terms = make_terms(where.astype(jnp.int32), own, other, jac_blocks[0, 0], cols)
    got = lax.all_to_all(terms, ROW, 0, 0)
    mine = add_up(got, faces)
    out = gather_result(mine).reshape(k, b, faces)
    return jnp.transpose(out, (2, 0, 1))


def solution(mesh):
    parts = Mesh(mesh.devices.reshape(SIZES), AXES)
    placed = (
        P(AXES, None, None),
        P(ROW, COL, None, None, None),
        P(ROW, COL, None),
        P(ROW, COL, None),
        P(ROW, COL),
    )
    return jax.shard_map(
        on_device, mesh=parts, in_specs=placed, out_specs=P(COL, None, None), check_vma=False
    )
```

```python
import jax
import jax.numpy as jnp
from jax import lax
from jax.experimental import pallas as pl
from jax.experimental.pallas import tpu as pltpu
from jax.sharding import Mesh, PartitionSpec as P


AXES = ("xlo", "z", "xhi", "y", "core")
SIZES = (2, 8, 2, 4, 2)
ROW = ("xlo", "z")
COL = ("xhi", "y", "core")

LANES = 128
DEPTH = 8
PITCH = 132
TERM_PITCH = 20
GROUP = 16
BITS = 15
LIMIT = 32767.0
TINY = 1e-30


def in_vmem():
    return pl.BlockSpec(memory_space=pltpu.VMEM)


def in_smem():
    return pl.BlockSpec(memory_space=pltpu.SMEM)


def params():
    return pltpu.CompilerParams(vmem_limit_bytes=24 << 20)


def flip_kernel(in_ref, out_ref):
    flipped = jnp.transpose(in_ref[...])
    for i in range(out_ref.shape[0]):
        out_ref[i] = flipped


def flip(faces, copies):
    rows, b = faces.shape
    return pl.pallas_call(
        flip_kernel,
        out_shape=pltpu.VMEM((copies, b, rows), faces.dtype),
        in_specs=[in_vmem()],
        out_specs=in_vmem(),
        compiler_params=params(),
        name="flip",
    )(faces)


def relayout_kernel(in_ref, out_ref, left_ref, right_ref):
    depth, b, slots = in_ref.shape
    for d in range(depth):
        block = in_ref[d].astype(jnp.float32)
        at = pl.ds(d * PITCH, slots)
        left_ref[at, :] = jnp.transpose(block[:LANES])
        right_ref[at, pl.ds(0, b - LANES)] = jnp.transpose(block[LANES:])
    for s in range(slots):
        at = pl.ds(s, depth, stride=PITCH)
        out_ref[s, :, pl.ds(0, LANES)] = left_ref[at, :].astype(jnp.bfloat16)
        out_ref[s, :, pl.ds(LANES, b - LANES)] = right_ref[at, :][:, : b - LANES].astype(jnp.bfloat16)


def relayout(jac):
    d, b, slots = jac.shape
    scratch = pltpu.VMEM((DEPTH * PITCH, LANES), jnp.float32)
    return pl.pallas_call(
        relayout_kernel,
        out_shape=pltpu.HBM((slots, d, b), jac.dtype),
        grid=(d // DEPTH,),
        in_specs=[pl.BlockSpec((DEPTH, b, slots), lambda i: (i, 0, 0))],
        out_specs=pl.BlockSpec((slots, DEPTH, b), lambda i: (0, i, 0)),
        scratch_shapes=[scratch, scratch],
        compiler_params=params(),
        name="relayout",
    )(pltpu.with_memory_space_constraint(jac, pltpu.HBM))


def pow2(exponent):
    return jnp.exp2(exponent).astype(jnp.bfloat16).astype(jnp.float32)


def terms_kernel(rows_ref, count_ref, cols_ref, own_ref, other_ref, jac_ref, out_ref, faces_ref, left_ref, right_ref):
    here, b, _ = jac_ref.shape
    k, _, slots = out_ref.shape
    pieces, _, per = own_ref.shape
    core = lax.axis_index("core")
    step = pl.program_id(0)

    @pl.when(step == 0)
    def _():
        for i in range(pieces):
            faces_ref[pl.ds(i * per, per), pl.ds(0, b)] = jnp.transpose(own_ref[i])
            faces_ref[pl.ds((pieces + i) * per, per), pl.ds(0, b)] = jnp.transpose(other_ref[i])

    for j in range(here):
        slot = step * here + j
        row = rows_ref[slot]
        home = row // k
        place = (((home & 1) ^ core) * pieces + home // 2) * per + (row & (k - 1)) * k
        lhs = faces_ref[pl.ds(pl.multiple_of(place, k), k), pl.ds(0, b)]
        term = jnp.dot(lhs, jac_ref[j], preferred_element_type=jnp.float32)
        at = pl.ds(pl.multiple_of(slot * TERM_PITCH, 4), k)
        left_ref[at, :] = term[:, :LANES]
        right_ref[at, pl.ds(0, b - LANES)] = term[:, LANES:]

    @pl.when(step == pl.num_programs(0) - 1)
    def _():
        meta_row = lax.broadcasted_iota(jnp.int32, (8, slots), 0)
        slot_index = lax.broadcasted_iota(jnp.int32, (1, slots), 1)
        cols = jnp.where(slot_index < count_ref[0, 0], cols_ref[...], -1).astype(jnp.float32)
        for i in range(k):
            at = pl.ds(i, slots, stride=TERM_PITCH)
            left = jnp.transpose(left_ref[at, :])
            right = jnp.transpose(right_ref[at, :])[: b - LANES]
            flipped = jnp.concatenate([left, right], axis=0)
            top = jnp.max(jnp.abs(flipped), axis=0, keepdims=True)
            exponent = jnp.ceil(jnp.log2(jnp.maximum(top, TINY)) + 0.01) - BITS
            scaled = jnp.clip(jnp.round(flipped * pow2(-exponent)), -LIMIT, LIMIT)
            meta = jnp.where(meta_row == 0, exponent, jnp.where(meta_row == 1, cols, 0.0))
            out_ref[i] = jnp.concatenate([scaled, meta], axis=0).astype(jnp.int32).astype(jnp.int16)


def make_terms(rows, count, cols, own, other, jac, k):
    slots, b, _ = jac.shape
    pieces, _, per = own.shape
    scratch = pltpu.VMEM((slots * TERM_PITCH, LANES), jnp.float32)
    return pl.pallas_call(
        terms_kernel,
        out_shape=pltpu.VMEM((k, b + 8, slots), jnp.int16),
        grid=(slots // GROUP,),
        in_specs=[in_smem(), in_smem(), in_vmem(), in_vmem(), in_vmem()]
        + [pl.BlockSpec((GROUP, b, b), lambda i: (i, 0, 0))],
        out_specs=in_vmem(),
        scratch_shapes=[pltpu.VMEM((2 * pieces * per, 2 * LANES), jnp.bfloat16), scratch, scratch],
        compiler_params=params(),
        name="terms",
    )(rows, count, cols, own, other, pltpu.with_memory_space_constraint(jac, pltpu.HBM))


def sum_kernel(got_ref, out_ref, lhs_ref, pick_ref):
    tiles, _, slots = got_ref.shape
    b, faces = out_ref.shape
    face = lax.broadcasted_iota(jnp.int32, (faces, slots), 0)
    for t in range(tiles):
        got = got_ref[t].astype(jnp.int32)
        high = got[:b] >> 8
        low = got[:b] & 255
        scale = pow2(got[b : b + 1].astype(jnp.float32))
        pick = jnp.where(face == got[b + 1 : b + 2], scale, 0.0)
        at = pl.ds(t * slots, slots)
        pick_ref[:, at] = pick.astype(jnp.bfloat16)
        lhs_ref[0:b, at] = (high.astype(jnp.float32) * 256.0).astype(jnp.bfloat16)
        lhs_ref[b : 2 * b, at] = low.astype(jnp.float32).astype(jnp.bfloat16)
    both = lax.dot_general(
        lhs_ref[...], pick_ref[...], (((1,), (1,)), ((), ())), preferred_element_type=jnp.float32
    )
    out_ref[...] = (both[:b] + both[b:]).astype(jnp.bfloat16)


def add_up(got, faces):
    tiles, rows, slots = got.shape
    b = rows - 8
    return pl.pallas_call(
        sum_kernel,
        out_shape=pltpu.VMEM((b, faces), jnp.bfloat16),
        in_specs=[in_vmem()],
        out_specs=in_vmem(),
        scratch_shapes=[
            pltpu.VMEM((2 * b, tiles * slots), jnp.bfloat16),
            pltpu.VMEM((faces, tiles * slots), jnp.bfloat16),
        ],
        compiler_params=params(),
        name="add_up",
    )(got)


def gather_result(mine):
    xlo = lax.axis_index("xlo")
    z = lax.axis_index("z")

    def up(piece):
        return lax.ppermute(piece, "z", [(i, (i + 1) % 8) for i in range(8)])

    def down(piece):
        return lax.ppermute(piece, "z", [(i, (i - 1) % 8) for i in range(8)])

    def across(piece):
        return lax.ppermute(piece, "xlo", [(0, 1), (1, 0)])

    held = {(0, 0): mine}
    held[0, -1], held[0, 1], held[1, 0] = up(mine), down(mine), across(mine)
    held[0, -2], held[0, 2], held[1, -1] = up(held[0, -1]), down(held[0, 1]), across(held[0, -1])
    held[0, -3], held[0, 3], held[1, 1] = up(held[0, -2]), down(held[0, 2]), across(held[0, 1])
    held[0, 4], held[1, 2], held[1, -2] = up(held[0, -3]), down(held[1, 1]), across(held[0, -2])
    held[1, -3], held[1, 3], held[1, 4] = up(held[1, -2]), down(held[1, 2]), across(held[0, 4])
    out = jnp.zeros((2, 8) + mine.shape, mine.dtype)
    for (x, d), piece in held.items():
        out = lax.dynamic_update_slice(out, piece[None, None], (xlo ^ x, (z + d + 8) % 8, 0, 0))
    return out


def on_device(adjoints, jac_blocks, jac_rows, jac_cols, tile_count):
    faces_here, k, b = adjoints.shape
    slots = jac_rows.shape[2]
    copies = flip(adjoints.reshape(faces_here * k, b), 8)
    own = lax.all_to_all(copies, ("xhi", "y"), 0, 0)
    other = lax.ppermute(own, "core", [(0, 1), (1, 0)])
    jac = relayout(jnp.transpose(jac_blocks[0, 0], (1, 2, 0)))
    terms = make_terms(jac_rows.reshape(slots), tile_count, jac_cols.reshape(1, slots), own, other, jac, k)
    got = lax.all_to_all(terms, ROW, 0, 0)
    mine = add_up(got, faces_here * 16)
    out = gather_result(mine).reshape(k, b, faces_here * 16)
    return jnp.transpose(out, (2, 0, 1))


def solution(mesh):
    parts = Mesh(mesh.devices.reshape(SIZES), AXES)
    placed = (
        P(AXES, None, None),
        P(ROW, COL, None, None, None),
        P(ROW, COL, None),
        P(ROW, COL, None),
        P(ROW, COL),
    )
    return jax.shard_map(
        on_device, mesh=parts, in_specs=placed, out_specs=P(COL, None, None), check_vma=False
    )
```

```python
import jax
import jax.numpy as jnp
from jax import lax
from jax.experimental import pallas as pl
from jax.experimental.pallas import tpu as pltpu
from jax.sharding import Mesh, PartitionSpec as P


AXES = ("xlo", "z", "xhi", "y", "core")
SIZES = (2, 8, 2, 4, 2)
ROW = ("xlo", "z")
COL = ("xhi", "y", "core")

LANES = 128
DEPTH = 8
CHUNKS = 5
PITCH = 132
TERM_PITCH = 20
GROUP = 16
BITS = 15
LIMIT = 32767.0
TINY = 1e-30


def in_vmem():
    return pl.BlockSpec(memory_space=pltpu.VMEM)


def in_smem():
    return pl.BlockSpec(memory_space=pltpu.SMEM)


def in_hbm(array):
    return pltpu.with_memory_space_constraint(array, pltpu.HBM)


def params(mib=16):
    return pltpu.CompilerParams(vmem_limit_bytes=mib << 20)


def flip_kernel(in_ref, out_ref):
    flipped = jnp.transpose(in_ref[...])
    for i in range(out_ref.shape[0]):
        out_ref[i] = flipped


def flip(faces, copies):
    rows, b = faces.shape
    return pl.pallas_call(
        flip_kernel,
        out_shape=pltpu.VMEM((copies, b, rows), faces.dtype),
        in_specs=[in_vmem()],
        out_specs=in_vmem(),
        compiler_params=params(),
        name="flip",
    )(faces)


def relayout_kernel(jac_ref, out_ref, in_buf, out_buf, left_ref, right_ref, in_sem, out_sem):
    chunks, many, b, slots = in_buf.shape

    def bring(c):
        return pltpu.make_async_copy(jac_ref.at[pl.ds(c * many, many)], in_buf.at[c], in_sem.at[c])

    def send(c):
        return pltpu.make_async_copy(out_buf.at[c], out_ref.at[:, pl.ds(c * many, many), :], out_sem.at[c])

    for c in range(chunks):
        bring(c).start()
    for c in range(chunks):
        bring(c).wait()

        def some(group, _):
            for d in range(DEPTH):
                block = in_buf[c, group * DEPTH + d].astype(jnp.float32)
                at = pl.ds(d * PITCH, slots)
                left_ref[at, :] = jnp.transpose(block[:LANES])
                right_ref[at, pl.ds(0, b - LANES)] = jnp.transpose(block[LANES:])
            rows = pl.ds(pl.multiple_of(group * DEPTH, DEPTH), DEPTH)
            for s in range(slots):
                at = pl.ds(s, DEPTH, stride=PITCH)
                out_buf[c, s, rows, pl.ds(0, LANES)] = left_ref[at, :].astype(jnp.bfloat16)
                out_buf[c, s, rows, pl.ds(LANES, b - LANES)] = right_ref[at, :][:, : b - LANES].astype(jnp.bfloat16)
            return 0

        lax.fori_loop(0, many // DEPTH, some, 0)
        send(c).start()
    for c in range(chunks):
        send(c).wait()


def relayout(jac):
    d, b, slots = jac.shape
    many = d // CHUNKS
    scratch = pltpu.VMEM((DEPTH * PITCH, LANES), jnp.float32)
    anywhere = pl.BlockSpec(memory_space=pltpu.HBM)
    return pl.pallas_call(
        relayout_kernel,
        out_shape=pltpu.HBM((slots, d, b), jac.dtype),
        in_specs=[anywhere],
        out_specs=anywhere,
        scratch_shapes=[
            pltpu.VMEM((CHUNKS, many, b, slots), jac.dtype),
            pltpu.VMEM((CHUNKS, slots, many, b), jac.dtype),
            scratch,
            scratch,
            pltpu.SemaphoreType.DMA((CHUNKS,)),
            pltpu.SemaphoreType.DMA((CHUNKS,)),
        ],
        compiler_params=params(40),
        name="relayout",
    )(in_hbm(jac))


def pow2(exponent):
    return jnp.exp2(exponent).astype(jnp.bfloat16).astype(jnp.float32)


def terms_kernel(
    rows_ref, count_ref, cols_ref, own_ref, other_ref, jac_ref, out_ref, jac_buf, faces_ref, left_ref, right_ref, sem
):
    slots, b, _ = jac_buf.shape
    k = out_ref.shape[0]
    pieces, _, per = own_ref.shape
    core = lax.axis_index("core")

    def bring(c):
        at = pl.ds(c * GROUP, GROUP)
        return pltpu.make_async_copy(jac_ref.at[at], jac_buf.at[at], sem.at[c])

    for c in range(slots // GROUP):
        bring(c).start()
    for i in range(pieces):
        faces_ref[pl.ds(i * per, per), pl.ds(0, b)] = jnp.transpose(own_ref[i])
        faces_ref[pl.ds((pieces + i) * per, per), pl.ds(0, b)] = jnp.transpose(other_ref[i])

    def some(c, _):
        bring(c).wait()
        for j in range(GROUP):
            slot = c * GROUP + j
            row = rows_ref[slot]
            home = row // k
            place = (((home & 1) ^ core) * pieces + home // 2) * per + (row & (k - 1)) * k
            lhs = faces_ref[pl.ds(pl.multiple_of(place, k), k), pl.ds(0, b)]
            term = jnp.dot(lhs, jac_buf[slot], preferred_element_type=jnp.float32)
            at = pl.ds(pl.multiple_of(slot * TERM_PITCH, 4), k)
            left_ref[at, :] = term[:, :LANES]
            right_ref[at, pl.ds(0, b - LANES)] = term[:, LANES:]
        return 0

    lax.fori_loop(0, slots // GROUP, some, 0)
    meta_row = lax.broadcasted_iota(jnp.int32, (8, slots), 0)
    slot_index = lax.broadcasted_iota(jnp.int32, (1, slots), 1)
    cols = jnp.where(slot_index < count_ref[0, 0], cols_ref[...], -1).astype(jnp.float32)
    for i in range(k):
        at = pl.ds(i, slots, stride=TERM_PITCH)
        left = jnp.transpose(left_ref[at, :])
        right = jnp.transpose(right_ref[at, :])[: b - LANES]
        flipped = jnp.concatenate([left, right], axis=0)
        top = jnp.max(jnp.abs(flipped), axis=0, keepdims=True)
        exponent = jnp.ceil(jnp.log2(jnp.maximum(top, TINY)) + 0.01) - BITS
        scaled = jnp.clip(jnp.round(flipped * pow2(-exponent)), -LIMIT, LIMIT)
        meta = jnp.where(meta_row == 0, exponent, jnp.where(meta_row == 1, cols, 0.0))
        out_ref[i] = jnp.concatenate([scaled, meta], axis=0).astype(jnp.int32).astype(jnp.int16)


def make_terms(rows, count, cols, own, other, jac, k):
    slots, b, _ = jac.shape
    pieces, _, per = own.shape
    scratch = pltpu.VMEM((slots * TERM_PITCH, LANES), jnp.float32)
    return pl.pallas_call(
        terms_kernel,
        out_shape=jax.ShapeDtypeStruct((k, b + 8, slots), jnp.int16),
        in_specs=[in_smem(), in_smem(), in_vmem(), in_vmem(), in_vmem(), pl.BlockSpec(memory_space=pltpu.HBM)],
        out_specs=in_vmem(),
        scratch_shapes=[
            pltpu.VMEM((slots, b, b), jac.dtype),
            pltpu.VMEM((2 * pieces * per, 2 * LANES), jnp.bfloat16),
            scratch,
            scratch,
            pltpu.SemaphoreType.DMA((slots // GROUP,)),
        ],
        compiler_params=params(32),
        name="terms",
    )(rows, count, cols, own, other, in_hbm(jac))


def sum_kernel(got_ref, out_ref, lhs_ref, pick_ref):
    tiles, _, slots = got_ref.shape
    b, faces = out_ref.shape
    face = lax.broadcasted_iota(jnp.int32, (faces, slots), 0)
    for t in range(tiles):
        got = got_ref[t].astype(jnp.int32)
        high = got[:b] >> 8
        low = got[:b] & 255
        scale = pow2(got[b : b + 1].astype(jnp.float32))
        pick = jnp.where(face == got[b + 1 : b + 2], scale, 0.0)
        at = pl.ds(t * slots, slots)
        pick_ref[:, at] = pick.astype(jnp.bfloat16)
        lhs_ref[0:b, at] = (high.astype(jnp.float32) * 256.0).astype(jnp.bfloat16)
        lhs_ref[b : 2 * b, at] = low.astype(jnp.float32).astype(jnp.bfloat16)
    both = lax.dot_general(
        lhs_ref[...], pick_ref[...], (((1,), (1,)), ((), ())), preferred_element_type=jnp.float32
    )
    out_ref[...] = (both[:b] + both[b:]).astype(jnp.bfloat16)


def add_up(got, faces):
    tiles, rows, slots = got.shape
    b = rows - 8
    return pl.pallas_call(
        sum_kernel,
        out_shape=pltpu.VMEM((b, faces), jnp.bfloat16),
        in_specs=[in_vmem()],
        out_specs=in_vmem(),
        scratch_shapes=[
            pltpu.VMEM((2 * b, tiles * slots), jnp.bfloat16),
            pltpu.VMEM((faces, tiles * slots), jnp.bfloat16),
        ],
        compiler_params=params(),
        name="add_up",
    )(got)


def gather_result(mine):
    xlo = lax.axis_index("xlo")
    z = lax.axis_index("z")

    def up(piece):
        return lax.ppermute(piece, "z", [(i, (i + 1) % 8) for i in range(8)])

    def down(piece):
        return lax.ppermute(piece, "z", [(i, (i - 1) % 8) for i in range(8)])

    def across(piece):
        return lax.ppermute(piece, "xlo", [(0, 1), (1, 0)])

    held = {(0, 0): mine}
    held[0, -1], held[0, 1], held[1, 0] = up(mine), down(mine), across(mine)
    held[0, -2], held[0, 2] = up(held[0, -1]), down(held[0, 1])
    held[1, -1], held[1, 1] = across(jnp.stack([held[0, -1], held[0, 1]]))
    held[0, -3], held[0, 3] = up(held[0, -2]), down(held[0, 2])
    held[1, -2], held[1, 2] = across(jnp.stack([held[0, -2], held[0, 2]]))
    held[1, -3], held[0, 4] = up(jnp.stack([held[1, -2], held[0, -3]]))
    held[1, 3] = down(held[1, 2])
    held[1, 4] = across(held[0, 4])
    out = jnp.zeros((2, 8) + mine.shape, mine.dtype)
    for (x, d), piece in held.items():
        out = lax.dynamic_update_slice(out, piece[None, None], (xlo ^ x, (z + d + 8) % 8, 0, 0))
    return out


def on_device(adjoints, jac_blocks, jac_rows, jac_cols, tile_count):
    faces_here, k, b = adjoints.shape
    slots = jac_rows.shape[2]
    copies = flip(adjoints.reshape(faces_here * k, b), 8)
    own = lax.all_to_all(copies, ("xhi", "y"), 0, 0)
    other = lax.ppermute(own, "core", [(0, 1), (1, 0)])
    jac = relayout(jnp.transpose(jac_blocks[0, 0], (1, 2, 0)))
    terms = make_terms(jac_rows.reshape(slots), tile_count, jac_cols.reshape(1, slots), own, other, jac, k)
    got = lax.all_to_all(terms, ROW, 0, 0)
    mine = add_up(got, faces_here * 16)
    out = gather_result(mine).reshape(k, b, faces_here * 16)
    return jnp.transpose(out, (2, 0, 1))


def solution(mesh):
    parts = Mesh(mesh.devices.reshape(SIZES), AXES)
    placed = (
        P(AXES, None, None),
        P(ROW, COL, None, None, None),
        P(ROW, COL, None),
        P(ROW, COL, None),
        P(ROW, COL),
    )
    return jax.shard_map(
        on_device, mesh=parts, in_specs=placed, out_specs=P(COL, None, None), check_vma=False
    )
```

```python
import jax
import jax.numpy as jnp
from jax import lax
from jax.experimental import pallas as pl
from jax.experimental.pallas import tpu as pltpu
from jax.sharding import Mesh, PartitionSpec as P


AXES = ("xlo", "z", "xhi", "y", "core")
SIZES = (2, 8, 2, 4, 2)
ROW = ("xlo", "z")
COL = ("xhi", "y", "core")

LANES = 128
DEPTH = 8
CHUNKS = 5
PITCH = 132
TERM_PITCH = 20
GROUP = 16
BITS = 15
LIMIT = 32767.0
TINY = 1e-30


def in_vmem():
    return pl.BlockSpec(memory_space=pltpu.VMEM)


def in_smem():
    return pl.BlockSpec(memory_space=pltpu.SMEM)


def in_hbm(array):
    return pltpu.with_memory_space_constraint(array, pltpu.HBM)


def params(mib=16):
    return pltpu.CompilerParams(vmem_limit_bytes=mib << 20)


def flip_kernel(in_ref, out_ref):
    flipped = jnp.transpose(in_ref[...])
    for i in range(out_ref.shape[0]):
        out_ref[i] = flipped


def flip(faces, copies):
    rows, b = faces.shape
    return pl.pallas_call(
        flip_kernel,
        out_shape=pltpu.VMEM((copies, b, rows), faces.dtype),
        in_specs=[in_vmem()],
        out_specs=in_vmem(),
        compiler_params=params(),
        name="flip",
    )(faces)


def relayout_kernel(jac_ref, out_ref, in_buf, out_buf, left_ref, right_ref, in_sem, out_sem):
    chunks, many, b, slots = in_buf.shape

    def bring(c):
        return pltpu.make_async_copy(jac_ref.at[pl.ds(c * many, many)], in_buf.at[c], in_sem.at[c])

    def send(c):
        return pltpu.make_async_copy(out_buf.at[c], out_ref.at[:, pl.ds(c * many, many), :], out_sem.at[c])

    for c in range(chunks):
        bring(c).start()
    for c in range(chunks):
        bring(c).wait()

        def some(group, _):
            for d in range(DEPTH):
                block = in_buf[c, group * DEPTH + d].astype(jnp.float32)
                at = pl.ds(d * PITCH, slots)
                left_ref[at, :] = jnp.transpose(block[:LANES])
                right_ref[at, pl.ds(0, b - LANES)] = jnp.transpose(block[LANES:])
            rows = pl.ds(pl.multiple_of(group * DEPTH, DEPTH), DEPTH)
            for s in range(slots):
                at = pl.ds(s, DEPTH, stride=PITCH)
                out_buf[c, s, rows, pl.ds(0, LANES)] = left_ref[at, :].astype(jnp.bfloat16)
                out_buf[c, s, rows, pl.ds(LANES, b - LANES)] = right_ref[at, :][:, : b - LANES].astype(jnp.bfloat16)
            return 0

        lax.fori_loop(0, many // DEPTH, some, 0)
        send(c).start()
    for c in range(chunks):
        send(c).wait()


def relayout(jac):
    d, b, slots = jac.shape
    many = d // CHUNKS
    scratch = pltpu.VMEM((DEPTH * PITCH, LANES), jnp.float32)
    anywhere = pl.BlockSpec(memory_space=pltpu.HBM)
    return pl.pallas_call(
        relayout_kernel,
        out_shape=pltpu.HBM((slots, d, b), jac.dtype),
        in_specs=[anywhere],
        out_specs=anywhere,
        scratch_shapes=[
            pltpu.VMEM((CHUNKS, many, b, slots), jac.dtype),
            pltpu.VMEM((CHUNKS, slots, many, b), jac.dtype),
            scratch,
            scratch,
            pltpu.SemaphoreType.DMA((CHUNKS,)),
            pltpu.SemaphoreType.DMA((CHUNKS,)),
        ],
        compiler_params=params(40),
        name="relayout",
    )(in_hbm(jac))


def pow2(exponent):
    return jnp.exp2(exponent).astype(jnp.bfloat16).astype(jnp.float32)


def terms_kernel(
    rows_ref, count_ref, cols_ref, own_ref, other_ref, jac_ref, out_ref, jac_buf, faces_ref, left_ref, right_ref, sem
):
    slots, b, _ = jac_buf.shape
    k = out_ref.shape[0]
    pieces, _, per = own_ref.shape
    core = lax.axis_index("core")

    def bring(c):
        at = pl.ds(c * GROUP, GROUP)
        return pltpu.make_async_copy(jac_ref.at[at], jac_buf.at[at], sem.at[c])

    for c in range(slots // GROUP):
        bring(c).start()
    for i in range(pieces):
        faces_ref[pl.ds(i * per, per), pl.ds(0, b)] = jnp.transpose(own_ref[i])
        faces_ref[pl.ds((pieces + i) * per, per), pl.ds(0, b)] = jnp.transpose(other_ref[i])

    def some(c, _):
        bring(c).wait()
        for j in range(GROUP):
            slot = c * GROUP + j
            row = rows_ref[slot]
            home = row // k
            place = (((home & 1) ^ core) * pieces + home // 2) * per + (row & (k - 1)) * k
            lhs = faces_ref[pl.ds(pl.multiple_of(place, k), k), pl.ds(0, b)]
            term = jnp.dot(lhs, jac_buf[slot], preferred_element_type=jnp.float32)
            at = pl.ds(pl.multiple_of(slot * TERM_PITCH, 4), k)
            left_ref[at, :] = term[:, :LANES]
            right_ref[at, pl.ds(0, b - LANES)] = term[:, LANES:]
        return 0

    lax.fori_loop(0, slots // GROUP, some, 0)
    meta_row = lax.broadcasted_iota(jnp.int32, (8, slots), 0)
    slot_index = lax.broadcasted_iota(jnp.int32, (1, slots), 1)
    cols = jnp.where(slot_index < count_ref[0, 0], cols_ref[...], -1).astype(jnp.float32)
    for i in range(k):
        at = pl.ds(i, slots, stride=TERM_PITCH)
        left = jnp.transpose(left_ref[at, :])
        right = jnp.transpose(right_ref[at, :])[: b - LANES]
        flipped = jnp.concatenate([left, right], axis=0)
        top = jnp.max(jnp.abs(flipped), axis=0, keepdims=True)
        exponent = jnp.ceil(jnp.log2(jnp.maximum(top, TINY)) + 0.01) - BITS
        scaled = jnp.clip(jnp.round(flipped * pow2(-exponent)), -LIMIT, LIMIT)
        meta = jnp.where(meta_row == 0, exponent, jnp.where(meta_row == 1, cols, 0.0))
        out_ref[i] = jnp.concatenate([scaled, meta], axis=0).astype(jnp.int32).astype(jnp.int16)


def make_terms(rows, count, cols, own, other, jac, k):
    slots, b, _ = jac.shape
    pieces, _, per = own.shape
    scratch = pltpu.VMEM((slots * TERM_PITCH, LANES), jnp.float32)
    return pl.pallas_call(
        terms_kernel,
        out_shape=jax.ShapeDtypeStruct((k, b + 8, slots), jnp.int16),
        in_specs=[in_smem(), in_smem(), in_vmem(), in_vmem(), in_vmem(), pl.BlockSpec(memory_space=pltpu.HBM)],
        out_specs=in_vmem(),
        scratch_shapes=[
            pltpu.VMEM((slots, b, b), jac.dtype),
            pltpu.VMEM((2 * pieces * per, 2 * LANES), jnp.bfloat16),
            scratch,
            scratch,
            pltpu.SemaphoreType.DMA((slots // GROUP,)),
        ],
        compiler_params=params(32),
        name="terms",
    )(rows, count, cols, own, other, in_hbm(jac))


def sum_kernel(got_ref, out_ref, lhs_ref, pick_ref):
    tiles, _, slots = got_ref.shape
    b, faces = out_ref.shape
    face = lax.broadcasted_iota(jnp.int32, (faces, slots), 0)
    for t in range(tiles):
        got = got_ref[t].astype(jnp.int32)
        high = got[:b] >> 8
        low = got[:b] & 255
        scale = pow2(got[b : b + 1].astype(jnp.float32))
        pick = jnp.where(face == got[b + 1 : b + 2], scale, 0.0)
        at = pl.ds(t * slots, slots)
        pick_ref[:, at] = pick.astype(jnp.bfloat16)
        lhs_ref[0:b, at] = (high.astype(jnp.float32) * 256.0).astype(jnp.bfloat16)
        lhs_ref[b : 2 * b, at] = low.astype(jnp.float32).astype(jnp.bfloat16)
    both = lax.dot_general(
        lhs_ref[...], pick_ref[...], (((1,), (1,)), ((), ())), preferred_element_type=jnp.float32
    )
    out_ref[...] = (both[:b] + both[b:]).astype(jnp.bfloat16)


def add_up(got, faces):
    tiles, rows, slots = got.shape
    b = rows - 8
    return pl.pallas_call(
        sum_kernel,
        out_shape=pltpu.VMEM((b, faces), jnp.bfloat16),
        in_specs=[in_vmem()],
        out_specs=in_vmem(),
        scratch_shapes=[
            pltpu.VMEM((2 * b, tiles * slots), jnp.bfloat16),
            pltpu.VMEM((faces, tiles * slots), jnp.bfloat16),
        ],
        compiler_params=params(),
        name="add_up",
    )(got)


def gather_result(mine):
    xlo = lax.axis_index("xlo")
    z = lax.axis_index("z")

    def up(piece):
        return lax.ppermute(piece, "z", [(i, (i + 1) % 8) for i in range(8)])

    def down(piece):
        return lax.ppermute(piece, "z", [(i, (i - 1) % 8) for i in range(8)])

    def across(piece):
        return lax.ppermute(piece, "xlo", [(0, 1), (1, 0)])

    def corner(piece):
        pairs = [(x * 8 + i, (1 - x) * 8 + (i + 1) % 8) for x in range(2) for i in range(8)]
        return lax.ppermute(piece, ROW, pairs)

    def both(one, two):
        return jnp.stack([one, two])

    held = {(0, 0): mine}
    held[0, -1], held[0, 1] = up(mine), down(mine)
    held[1, 0] = across(mine)
    held[0, -2], held[0, 2] = up(held[0, -1]), down(held[0, 1])
    held[1, -1], held[1, 1] = across(both(held[0, -1], held[0, 1]))
    held[0, -3], held[0, 3] = up(held[0, -2]), down(held[0, 2])
    held[1, -2], held[1, 2] = across(both(held[0, -2], held[0, 2]))
    held[1, -3], held[1, 3] = across(both(held[0, -3], held[0, 3]))
    held[0, 4] = down(held[0, 3])
    held[1, -4] = corner(held[0, -3])
    out = jnp.zeros((2, 8) + mine.shape, mine.dtype)
    for (x, d), piece in held.items():
        out = lax.dynamic_update_slice(out, piece[None, None], (xlo ^ x, (z + d + 8) % 8, 0, 0))
    return out


def on_device(adjoints, jac_blocks, jac_rows, jac_cols, tile_count):
    faces_here, k, b = adjoints.shape
    slots = jac_rows.shape[2]
    copies = flip(adjoints.reshape(faces_here * k, b), 8)
    own = lax.all_to_all(copies, ("xhi", "y"), 0, 0)
    other = lax.ppermute(own, "core", [(0, 1), (1, 0)])
    jac = relayout(jnp.transpose(jac_blocks[0, 0], (1, 2, 0)))
    terms = make_terms(jac_rows.reshape(slots), tile_count, jac_cols.reshape(1, slots), own, other, jac, k)
    got = lax.all_to_all(terms, ROW, 0, 0)
    mine = add_up(got, faces_here * 16)
    out = gather_result(mine).reshape(k, b, faces_here * 16)
    return jnp.transpose(out, (2, 0, 1))


def solution(mesh):
    parts = Mesh(mesh.devices.reshape(SIZES), AXES)
    placed = (
        P(AXES, None, None),
        P(ROW, COL, None, None, None),
        P(ROW, COL, None),
        P(ROW, COL, None),
        P(ROW, COL),
    )
    return jax.shard_map(
        on_device, mesh=parts, in_specs=placed, out_specs=P(COL, None, None), check_vma=False
    )
```

```python
import jax
import jax.numpy as jnp
from jax import lax
from jax.experimental import pallas as pl
from jax.experimental.pallas import tpu as pltpu
from jax.sharding import Mesh, PartitionSpec as P


AXES = ("xlo", "z", "xhi", "y", "core")
SIZES = (2, 8, 2, 4, 2)
ROW = ("xlo", "z")
COL = ("xhi", "y", "core")

LANES = 128
DEPTH = 8
CHUNKS = 5
PITCH = 132
TERM_PITCH = 20
GROUP = 16
BITS = 15
LIMIT = 32767.0
TINY = 1e-30


def in_vmem():
    return pl.BlockSpec(memory_space=pltpu.VMEM)


def in_smem():
    return pl.BlockSpec(memory_space=pltpu.SMEM)


def in_hbm(array):
    return pltpu.with_memory_space_constraint(array, pltpu.HBM)


def params(mib=16):
    return pltpu.CompilerParams(vmem_limit_bytes=mib << 20)


def flip_kernel(in_ref, out_ref, in_buf, out_buf, in_sem, out_sem):
    bring = pltpu.make_async_copy(in_ref, in_buf, in_sem)
    bring.start()
    bring.wait()
    out_buf[...] = jnp.transpose(in_buf[...])

    def send(i):
        return pltpu.make_async_copy(out_buf, out_ref.at[i], out_sem.at[i])

    copies = out_ref.shape[0]
    for i in range(copies):
        send(i).start()
    for i in range(copies):
        send(i).wait()


def flip(faces, copies):
    rows, b = faces.shape
    anywhere = pl.BlockSpec(memory_space=pltpu.HBM)
    return pl.pallas_call(
        flip_kernel,
        out_shape=pltpu.HBM((copies, b, rows), faces.dtype),
        in_specs=[anywhere],
        out_specs=anywhere,
        scratch_shapes=[
            pltpu.VMEM((rows, b), faces.dtype),
            pltpu.VMEM((b, rows), faces.dtype),
            pltpu.SemaphoreType.DMA,
            pltpu.SemaphoreType.DMA((copies,)),
        ],
        compiler_params=params(),
        name="flip",
    )(in_hbm(faces))


def relayout_kernel(jac_ref, out_ref, in_buf, out_buf, left_ref, right_ref, in_sem, out_sem):
    chunks, many, b, slots = in_buf.shape

    def bring(c):
        return pltpu.make_async_copy(jac_ref.at[pl.ds(c * many, many)], in_buf.at[c], in_sem.at[c])

    def send(c):
        return pltpu.make_async_copy(out_buf.at[c], out_ref.at[:, pl.ds(c * many, many), :], out_sem.at[c])

    for c in range(chunks):
        bring(c).start()
    for c in range(chunks):
        bring(c).wait()

        def some(group, _):
            for d in range(DEPTH):
                block = in_buf[c, group * DEPTH + d].astype(jnp.float32)
                at = pl.ds(d * PITCH, slots)
                left_ref[at, :] = jnp.transpose(block[:LANES])
                right_ref[at, pl.ds(0, b - LANES)] = jnp.transpose(block[LANES:])
            rows = pl.ds(pl.multiple_of(group * DEPTH, DEPTH), DEPTH)
            for s in range(slots):
                at = pl.ds(s, DEPTH, stride=PITCH)
                out_buf[c, s, rows, pl.ds(0, LANES)] = left_ref[at, :].astype(jnp.bfloat16)
                out_buf[c, s, rows, pl.ds(LANES, b - LANES)] = right_ref[at, :][:, : b - LANES].astype(jnp.bfloat16)
            return 0

        lax.fori_loop(0, many // DEPTH, some, 0)
        send(c).start()
    for c in range(chunks):
        send(c).wait()


def relayout(jac):
    d, b, slots = jac.shape
    many = d // CHUNKS
    scratch = pltpu.VMEM((DEPTH * PITCH, LANES), jnp.float32)
    anywhere = pl.BlockSpec(memory_space=pltpu.HBM)
    return pl.pallas_call(
        relayout_kernel,
        out_shape=pltpu.HBM((slots, d, b), jac.dtype),
        in_specs=[anywhere],
        out_specs=anywhere,
        scratch_shapes=[
            pltpu.VMEM((CHUNKS, many, b, slots), jac.dtype),
            pltpu.VMEM((CHUNKS, slots, many, b), jac.dtype),
            scratch,
            scratch,
            pltpu.SemaphoreType.DMA((CHUNKS,)),
            pltpu.SemaphoreType.DMA((CHUNKS,)),
        ],
        compiler_params=params(40),
        name="relayout",
    )(in_hbm(jac))


def pow2(exponent):
    return jnp.exp2(exponent).astype(jnp.bfloat16).astype(jnp.float32)


def terms_kernel(
    rows_ref, count_ref, cols_ref, own_ref, other_ref, jac_ref, out_ref, jac_buf, faces_ref, left_ref, right_ref, out_buf, sem, out_sem
):
    slots, b, _ = jac_buf.shape
    k = out_buf.shape[0]
    pieces, _, per = own_ref.shape
    core = lax.axis_index("core")

    def bring(c):
        at = pl.ds(c * GROUP, GROUP)
        return pltpu.make_async_copy(jac_ref.at[at], jac_buf.at[at], sem.at[c])

    def send(i):
        return pltpu.make_async_copy(out_buf.at[i], out_ref.at[i], out_sem.at[i])

    for c in range(slots // GROUP):
        bring(c).start()
    for i in range(pieces):
        faces_ref[pl.ds(i * per, per), pl.ds(0, b)] = jnp.transpose(own_ref[i])
        faces_ref[pl.ds((pieces + i) * per, per), pl.ds(0, b)] = jnp.transpose(other_ref[i])

    def some(c, _):
        bring(c).wait()
        for j in range(GROUP):
            slot = c * GROUP + j
            row = rows_ref[slot]
            home = row // k
            place = (((home & 1) ^ core) * pieces + home // 2) * per + (row & (k - 1)) * k
            lhs = faces_ref[pl.ds(pl.multiple_of(place, k), k), pl.ds(0, b)]
            term = jnp.dot(lhs, jac_buf[slot], preferred_element_type=jnp.float32)
            at = pl.ds(pl.multiple_of(slot * TERM_PITCH, 4), k)
            left_ref[at, :] = term[:, :LANES]
            right_ref[at, pl.ds(0, b - LANES)] = term[:, LANES:]
        return 0

    lax.fori_loop(0, slots // GROUP, some, 0)
    meta_row = lax.broadcasted_iota(jnp.int32, (8, slots), 0)
    slot_index = lax.broadcasted_iota(jnp.int32, (1, slots), 1)
    cols = jnp.where(slot_index < count_ref[0, 0], cols_ref[...], -1).astype(jnp.float32)
    for i in range(k):
        at = pl.ds(i, slots, stride=TERM_PITCH)
        left = jnp.transpose(left_ref[at, :])
        right = jnp.transpose(right_ref[at, :])[: b - LANES]
        flipped = jnp.concatenate([left, right], axis=0)
        top = jnp.max(jnp.abs(flipped), axis=0, keepdims=True)
        exponent = jnp.ceil(jnp.log2(jnp.maximum(top, TINY)) + 0.01) - BITS
        scaled = jnp.clip(jnp.round(flipped * pow2(-exponent)), -LIMIT, LIMIT)
        meta = jnp.where(meta_row == 0, exponent, jnp.where(meta_row == 1, cols, 0.0))
        out_buf[i] = jnp.concatenate([scaled, meta], axis=0).astype(jnp.int32).astype(jnp.int16)
        send(i).start()
    for i in range(k):
        send(i).wait()


def make_terms(rows, count, cols, own, other, jac, k):
    slots, b, _ = jac.shape
    pieces, _, per = own.shape
    scratch = pltpu.VMEM((slots * TERM_PITCH, LANES), jnp.float32)
    return pl.pallas_call(
        terms_kernel,
        out_shape=pltpu.HBM((k, b + 8, slots), jnp.int16),
        in_specs=[in_smem(), in_smem(), in_vmem(), in_vmem(), in_vmem(), pl.BlockSpec(memory_space=pltpu.HBM)],
        out_specs=pl.BlockSpec(memory_space=pltpu.HBM),
        scratch_shapes=[
            pltpu.VMEM((slots, b, b), jac.dtype),
            pltpu.VMEM((2 * pieces * per, 2 * LANES), jnp.bfloat16),
            scratch,
            scratch,
            pltpu.VMEM((k, b + 8, slots), jnp.int16),
            pltpu.SemaphoreType.DMA((slots // GROUP,)),
            pltpu.SemaphoreType.DMA((k,)),
        ],
        compiler_params=params(32),
        name="terms",
    )(rows, count, cols, own, other, in_hbm(jac))


def sum_kernel(got_ref, out_ref, lhs_ref, pick_ref):
    tiles, _, slots = got_ref.shape
    b, faces = out_ref.shape
    face = lax.broadcasted_iota(jnp.int32, (faces, slots), 0)
    for t in range(tiles):
        got = got_ref[t].astype(jnp.int32)
        high = got[:b] >> 8
        low = got[:b] & 255
        scale = pow2(got[b : b + 1].astype(jnp.float32))
        pick = jnp.where(face == got[b + 1 : b + 2], scale, 0.0)
        at = pl.ds(t * slots, slots)
        pick_ref[:, at] = pick.astype(jnp.bfloat16)
        lhs_ref[0:b, at] = (high.astype(jnp.float32) * 256.0).astype(jnp.bfloat16)
        lhs_ref[b : 2 * b, at] = low.astype(jnp.float32).astype(jnp.bfloat16)
    both = lax.dot_general(
        lhs_ref[...], pick_ref[...], (((1,), (1,)), ((), ())), preferred_element_type=jnp.float32
    )
    out_ref[...] = (both[:b] + both[b:]).astype(jnp.bfloat16)


def add_up(got, faces):
    tiles, rows, slots = got.shape
    b = rows - 8
    return pl.pallas_call(
        sum_kernel,
        out_shape=pltpu.VMEM((b, faces), jnp.bfloat16),
        in_specs=[in_vmem()],
        out_specs=in_vmem(),
        scratch_shapes=[
            pltpu.VMEM((2 * b, tiles * slots), jnp.bfloat16),
            pltpu.VMEM((faces, tiles * slots), jnp.bfloat16),
        ],
        compiler_params=params(),
        name="add_up",
    )(got)


def gather_result(mine):
    xlo = lax.axis_index("xlo")
    z = lax.axis_index("z")

    def up(piece):
        return lax.ppermute(piece, "z", [(i, (i + 1) % 8) for i in range(8)])

    def down(piece):
        return lax.ppermute(piece, "z", [(i, (i - 1) % 8) for i in range(8)])

    def across(piece):
        return lax.ppermute(piece, "xlo", [(0, 1), (1, 0)])

    def corner(piece):
        pairs = [(x * 8 + i, (1 - x) * 8 + (i + 1) % 8) for x in range(2) for i in range(8)]
        return lax.ppermute(piece, ROW, pairs)

    def both(one, two):
        return jnp.stack([one, two])

    held = {(0, 0): mine}
    held[0, -1], held[0, 1] = up(mine), down(mine)
    held[1, 0] = across(mine)
    held[0, -2], held[0, 2] = up(held[0, -1]), down(held[0, 1])
    held[1, -1], held[1, 1] = across(both(held[0, -1], held[0, 1]))
    held[0, -3], held[0, 3] = up(held[0, -2]), down(held[0, 2])
    held[1, -2], held[1, 2] = across(both(held[0, -2], held[0, 2]))
    held[1, -4] = corner(held[0, -3])
    held[0, 4] = down(held[0, 3])
    held[1, 3] = across(held[0, 3])
    held[1, -3] = up(held[1, -2])
    out = jnp.zeros((2, 8) + mine.shape, mine.dtype)
    for (x, d), piece in held.items():
        out = lax.dynamic_update_slice(out, piece[None, None], (xlo ^ x, (z + d + 8) % 8, 0, 0))
    return out


def on_device(adjoints, jac_blocks, jac_rows, jac_cols, tile_count):
    faces_here, k, b = adjoints.shape
    slots = jac_rows.shape[2]
    copies = flip(adjoints.reshape(faces_here * k, b), 8)
    own = lax.all_to_all(copies, ("xhi", "y"), 0, 0)
    other = lax.ppermute(own, "core", [(0, 1), (1, 0)])
    jac = relayout(jnp.transpose(jac_blocks[0, 0], (1, 2, 0)))
    terms = make_terms(jac_rows.reshape(slots), tile_count, jac_cols.reshape(1, slots), own, other, jac, k)
    got = lax.all_to_all(terms, ROW, 0, 0)
    mine = add_up(got, faces_here * 16)
    out = gather_result(mine).reshape(k, b, faces_here * 16)
    return jnp.transpose(out, (2, 0, 1))


def solution(mesh):
    parts = Mesh(mesh.devices.reshape(SIZES), AXES)
    placed = (
        P(AXES, None, None),
        P(ROW, COL, None, None, None),
        P(ROW, COL, None),
        P(ROW, COL, None),
        P(ROW, COL),
    )
    return jax.shard_map(
        on_device, mesh=parts, in_specs=placed, out_specs=P(COL, None, None), check_vma=False
    )
```

```python
import jax
import jax.numpy as jnp
from jax import lax
from jax.experimental import pallas as pl
from jax.experimental.pallas import tpu as pltpu
from jax.sharding import Mesh, PartitionSpec as P


AXES = ("xlo", "z", "xhi", "y", "core")
SIZES = (2, 8, 2, 4, 2)
ROW = ("xlo", "z")
COL = ("xhi", "y", "core")

LANES = 128
DEPTH = 8
CHUNKS = 5
PITCH = 132
TERM_PITCH = 20
GROUP = 16
BITS = 15
LIMIT = 32767.0
TINY = 1e-30


def in_vmem():
    return pl.BlockSpec(memory_space=pltpu.VMEM)


def in_smem():
    return pl.BlockSpec(memory_space=pltpu.SMEM)


def in_hbm(array):
    return pltpu.with_memory_space_constraint(array, pltpu.HBM)


def params(mib=16):
    return pltpu.CompilerParams(vmem_limit_bytes=mib << 20)


def flip_kernel(in_ref, out_ref, in_buf, out_buf, in_sem, out_sem):
    bring = pltpu.make_async_copy(in_ref, in_buf, in_sem)
    bring.start()
    bring.wait()
    out_buf[...] = jnp.transpose(in_buf[...])

    def send(i):
        return pltpu.make_async_copy(out_buf, out_ref.at[i], out_sem.at[i])

    copies = out_ref.shape[0]
    for i in range(copies):
        send(i).start()
    for i in range(copies):
        send(i).wait()


def flip(faces, copies):
    rows, b = faces.shape
    anywhere = pl.BlockSpec(memory_space=pltpu.HBM)
    return pl.pallas_call(
        flip_kernel,
        out_shape=pltpu.HBM((copies, b, rows), faces.dtype),
        in_specs=[anywhere],
        out_specs=anywhere,
        scratch_shapes=[
            pltpu.VMEM((rows, b), faces.dtype),
            pltpu.VMEM((b, rows), faces.dtype),
            pltpu.SemaphoreType.DMA,
            pltpu.SemaphoreType.DMA((copies,)),
        ],
        compiler_params=params(),
        name="flip",
    )(in_hbm(faces))


def relayout_kernel(jac_ref, out_ref, in_buf, out_buf, left_ref, right_ref, in_sem, out_sem):
    chunks, many, b, slots = in_buf.shape

    def bring(c):
        return pltpu.make_async_copy(jac_ref.at[pl.ds(c * many, many)], in_buf.at[c], in_sem.at[c])

    def send(c):
        return pltpu.make_async_copy(out_buf.at[c], out_ref.at[:, pl.ds(c * many, many), :], out_sem.at[c])

    for c in range(chunks):
        bring(c).start()
    for c in range(chunks):
        bring(c).wait()

        def some(group, _):
            for d in range(DEPTH):
                block = in_buf[c, group * DEPTH + d].astype(jnp.float32)
                at = pl.ds(d * PITCH, slots)
                left_ref[at, :] = jnp.transpose(block[:LANES])
                right_ref[at, pl.ds(0, b - LANES)] = jnp.transpose(block[LANES:])
            rows = pl.ds(pl.multiple_of(group * DEPTH, DEPTH), DEPTH)
            for s in range(slots):
                at = pl.ds(s, DEPTH, stride=PITCH)
                out_buf[c, s, rows, pl.ds(0, LANES)] = left_ref[at, :].astype(jnp.bfloat16)
                out_buf[c, s, rows, pl.ds(LANES, b - LANES)] = right_ref[at, :][:, : b - LANES].astype(jnp.bfloat16)
            return 0

        lax.fori_loop(0, many // DEPTH, some, 0)
        send(c).start()
    for c in range(chunks):
        send(c).wait()


def relayout(jac):
    d, b, slots = jac.shape
    many = d // CHUNKS
    scratch = pltpu.VMEM((DEPTH * PITCH, LANES), jnp.float32)
    anywhere = pl.BlockSpec(memory_space=pltpu.HBM)
    return pl.pallas_call(
        relayout_kernel,
        out_shape=pltpu.HBM((slots, d, b), jac.dtype),
        in_specs=[anywhere],
        out_specs=anywhere,
        scratch_shapes=[
            pltpu.VMEM((CHUNKS, many, b, slots), jac.dtype),
            pltpu.VMEM((CHUNKS, slots, many, b), jac.dtype),
            scratch,
            scratch,
            pltpu.SemaphoreType.DMA((CHUNKS,)),
            pltpu.SemaphoreType.DMA((CHUNKS,)),
        ],
        compiler_params=params(40),
        name="relayout",
    )(in_hbm(jac))


def pow2(exponent):
    return jnp.exp2(exponent).astype(jnp.bfloat16).astype(jnp.float32)


def terms_kernel(
    rows_ref, count_ref, cols_ref, own_ref, other_ref, jac_ref, out_ref, jac_buf, faces_ref, left_ref, right_ref, out_buf, sem, out_sem
):
    slots, b, _ = jac_buf.shape
    k = out_buf.shape[0]
    pieces, _, per = own_ref.shape
    core = lax.axis_index("core")

    def bring(c):
        at = pl.ds(c * GROUP, GROUP)
        return pltpu.make_async_copy(jac_ref.at[at], jac_buf.at[at], sem.at[c])

    def send(i):
        return pltpu.make_async_copy(out_buf.at[i], out_ref.at[i], out_sem.at[i])

    for c in range(slots // GROUP):
        bring(c).start()
    for i in range(pieces):
        faces_ref[pl.ds(i * per, per), pl.ds(0, b)] = jnp.transpose(own_ref[i])
        faces_ref[pl.ds((pieces + i) * per, per), pl.ds(0, b)] = jnp.transpose(other_ref[i])

    def some(c, _):
        bring(c).wait()
        for j in range(GROUP):
            slot = c * GROUP + j
            row = rows_ref[slot]
            home = row // k
            owner = home & 1
            piece = (home // 2) ^ (owner * (pieces - 1))
            place = ((owner ^ core) * pieces + piece) * per + (row & (k - 1)) * k
            lhs = faces_ref[pl.ds(pl.multiple_of(place, k), k), pl.ds(0, b)]
            term = jnp.dot(lhs, jac_buf[slot], preferred_element_type=jnp.float32)
            at = pl.ds(pl.multiple_of(slot * TERM_PITCH, 4), k)
            left_ref[at, :] = term[:, :LANES]
            right_ref[at, pl.ds(0, b - LANES)] = term[:, LANES:]
        return 0

    lax.fori_loop(0, slots // GROUP, some, 0)
    meta_row = lax.broadcasted_iota(jnp.int32, (8, slots), 0)
    slot_index = lax.broadcasted_iota(jnp.int32, (1, slots), 1)
    cols = jnp.where(slot_index < count_ref[0, 0], cols_ref[...], -1).astype(jnp.float32)
    for i in range(k):
        at = pl.ds(i, slots, stride=TERM_PITCH)
        left = jnp.transpose(left_ref[at, :])
        right = jnp.transpose(right_ref[at, :])[: b - LANES]
        flipped = jnp.concatenate([left, right], axis=0)
        top = jnp.max(jnp.abs(flipped), axis=0, keepdims=True)
        exponent = jnp.ceil(jnp.log2(jnp.maximum(top, TINY)) + 0.01) - BITS
        scaled = jnp.clip(jnp.round(flipped * pow2(-exponent)), -LIMIT, LIMIT)
        meta = jnp.where(meta_row == 0, exponent, jnp.where(meta_row == 1, cols, 0.0))
        out_buf[i] = jnp.concatenate([scaled, meta], axis=0).astype(jnp.int32).astype(jnp.int16)
        send(i).start()
    for i in range(k):
        send(i).wait()


def make_terms(rows, count, cols, own, other, jac, k):
    slots, b, _ = jac.shape
    pieces, _, per = own.shape
    scratch = pltpu.VMEM((slots * TERM_PITCH, LANES), jnp.float32)
    return pl.pallas_call(
        terms_kernel,
        out_shape=pltpu.HBM((k, b + 8, slots), jnp.int16),
        in_specs=[in_smem(), in_smem(), in_vmem(), in_vmem(), in_vmem(), pl.BlockSpec(memory_space=pltpu.HBM)],
        out_specs=pl.BlockSpec(memory_space=pltpu.HBM),
        scratch_shapes=[
            pltpu.VMEM((slots, b, b), jac.dtype),
            pltpu.VMEM((2 * pieces * per, 2 * LANES), jnp.bfloat16),
            scratch,
            scratch,
            pltpu.VMEM((k, b + 8, slots), jnp.int16),
            pltpu.SemaphoreType.DMA((slots // GROUP,)),
            pltpu.SemaphoreType.DMA((k,)),
        ],
        compiler_params=params(32),
        name="terms",
    )(rows, count, cols, own, other, in_hbm(jac))


def sum_kernel(got_ref, out_ref, lhs_ref, pick_ref):
    tiles, _, slots = got_ref.shape
    b, faces = out_ref.shape
    face = lax.broadcasted_iota(jnp.int32, (faces, slots), 0)
    for t in range(tiles):
        got = got_ref[t].astype(jnp.int32)
        high = got[:b] >> 8
        low = got[:b] & 255
        scale = pow2(got[b : b + 1].astype(jnp.float32))
        pick = jnp.where(face == got[b + 1 : b + 2], scale, 0.0)
        at = pl.ds(t * slots, slots)
        pick_ref[:, at] = pick.astype(jnp.bfloat16)
        lhs_ref[0:b, at] = (high.astype(jnp.float32) * 256.0).astype(jnp.bfloat16)
        lhs_ref[b : 2 * b, at] = low.astype(jnp.float32).astype(jnp.bfloat16)
    both = lax.dot_general(
        lhs_ref[...], pick_ref[...], (((1,), (1,)), ((), ())), preferred_element_type=jnp.float32
    )
    out_ref[...] = (both[:b] + both[b:]).astype(jnp.bfloat16)


def add_up(got, faces):
    tiles, rows, slots = got.shape
    b = rows - 8
    return pl.pallas_call(
        sum_kernel,
        out_shape=pltpu.VMEM((b, faces), jnp.bfloat16),
        in_specs=[in_vmem()],
        out_specs=in_vmem(),
        scratch_shapes=[
            pltpu.VMEM((2 * b, tiles * slots), jnp.bfloat16),
            pltpu.VMEM((faces, tiles * slots), jnp.bfloat16),
        ],
        compiler_params=params(),
        name="add_up",
    )(got)


def both_ways(groups):
    return [[2 * i for i in groups], [2 * i + 1 for i in reversed(groups)]]


def gather_result(mine):
    xlo = lax.axis_index("xlo")
    z = lax.axis_index("z")
    core = lax.axis_index("core")

    def shift(turn, cross):
        steps = (turn, -turn)
        return [
            (x * 16 + i * 2 + c, (x ^ cross) * 16 + (i + steps[c]) % 8 * 2 + c)
            for x in range(2)
            for i in range(8)
            for c in range(2)
        ]

    def send(piece, turn, cross):
        return lax.ppermute(piece, ("xlo", "z", "core"), shift(turn, cross))

    def up(piece):
        return send(piece, 1, 0)

    def down(piece):
        return send(piece, -1, 0)

    def across(piece):
        return send(piece, 0, 1)

    def both(one, two):
        return jnp.stack([one, two])

    held = {(0, 0): mine}
    held[0, -1], held[0, 1] = up(mine), down(mine)
    held[1, 0] = across(mine)
    held[0, -2], held[0, 2] = up(held[0, -1]), down(held[0, 1])
    held[1, -1], held[1, 1] = across(both(held[0, -1], held[0, 1]))
    held[0, -3], held[0, 3] = up(held[0, -2]), down(held[0, 2])
    held[1, -2], held[1, 2] = across(both(held[0, -2], held[0, 2]))
    held[1, -3], held[1, 3] = across(both(held[0, -3], held[0, 3]))
    held[0, 4] = down(held[0, 3])
    held[1, -4] = send(held[0, -3], 1, 1)
    out = jnp.zeros((2, 8) + mine.shape, mine.dtype)
    for (x, d), piece in held.items():
        at = (z + (1 - 2 * core) * d + 8) % 8
        out = lax.dynamic_update_slice(out, piece[None, None], (xlo ^ x ^ core, at ^ (7 * core), 0, 0))
    return out


def on_device(adjoints, jac_blocks, jac_rows, jac_cols, tile_count):
    faces_here, k, b = adjoints.shape
    slots = jac_rows.shape[2]
    copies = flip(adjoints.reshape(faces_here * k, b), 8)
    own = lax.all_to_all(copies, COL, 0, 0, axis_index_groups=both_ways(range(8)))
    other = lax.ppermute(own, "core", [(0, 1), (1, 0)])
    jac = relayout(jnp.transpose(jac_blocks[0, 0], (1, 2, 0)))
    terms = make_terms(jac_rows.reshape(slots), tile_count, jac_cols.reshape(1, slots), own, other, jac, k)
    got = lax.all_to_all(terms, ROW + ("core",), 0, 0, axis_index_groups=both_ways(range(16)))
    mine = add_up(got, faces_here * 16)
    out = gather_result(mine).reshape(k, b, faces_here * 16)
    return jnp.transpose(out, (2, 0, 1))


def solution(mesh):
    parts = Mesh(mesh.devices.reshape(SIZES), AXES)
    placed = (
        P(AXES, None, None),
        P(ROW, COL, None, None, None),
        P(ROW, COL, None),
        P(ROW, COL, None),
        P(ROW, COL),
    )
    return jax.shard_map(
        on_device, mesh=parts, in_specs=placed, out_specs=P(COL, None, None), check_vma=False
    )
```

```python
import jax
import jax.numpy as jnp
from jax import lax
from jax.experimental import pallas as pl
from jax.experimental.pallas import tpu as pltpu
from jax.sharding import Mesh, PartitionSpec as P


AXES = ("xlo", "z", "xhi", "y", "core")
SIZES = (2, 8, 2, 4, 2)
ROW = ("xlo", "z")
COL = ("xhi", "y", "core")

LANES = 128
DEPTH = 8
CHUNKS = 5
PITCH = 132
TERM_PITCH = 20
GROUP = 16
BITS = 15
LIMIT = 32767.0
TINY = 1e-30


def in_vmem():
    return pl.BlockSpec(memory_space=pltpu.VMEM)


def in_smem():
    return pl.BlockSpec(memory_space=pltpu.SMEM)


def in_hbm(array):
    return pltpu.with_memory_space_constraint(array, pltpu.HBM)


def params(mib=16):
    return pltpu.CompilerParams(vmem_limit_bytes=mib << 20)


def flip_kernel(in_ref, out_ref, in_buf, out_buf, in_sem, out_sem):
    bring = pltpu.make_async_copy(in_ref, in_buf, in_sem)
    bring.start()
    bring.wait()
    out_buf[...] = jnp.transpose(in_buf[...])

    def send(i):
        return pltpu.make_async_copy(out_buf, out_ref.at[i], out_sem.at[i])

    copies = out_ref.shape[0]
    for i in range(copies):
        send(i).start()
    for i in range(copies):
        send(i).wait()


def flip(faces, copies):
    rows, b = faces.shape
    anywhere = pl.BlockSpec(memory_space=pltpu.HBM)
    return pl.pallas_call(
        flip_kernel,
        out_shape=pltpu.HBM((copies, b, rows), faces.dtype),
        in_specs=[anywhere],
        out_specs=anywhere,
        scratch_shapes=[
            pltpu.VMEM((rows, b), faces.dtype),
            pltpu.VMEM((b, rows), faces.dtype),
            pltpu.SemaphoreType.DMA,
            pltpu.SemaphoreType.DMA((copies,)),
        ],
        compiler_params=params(),
        name="flip",
    )(in_hbm(faces))


def relayout_kernel(jac_ref, out_ref, in_buf, out_buf, left_ref, right_ref, in_sem, out_sem):
    groups, _, b, slots = in_buf.shape
    chunks, _, many, _ = out_buf.shape
    per_chunk = many // DEPTH
    head = per_chunk // 2 * DEPTH

    def bring(g):
        return pltpu.make_async_copy(jac_ref.at[pl.ds(g * DEPTH, DEPTH)], in_buf.at[g], in_sem.at[g])

    def send(c, start, count, sem):
        at = pl.ds(c * many + start, count)
        return pltpu.make_async_copy(out_buf.at[c, :, pl.ds(start, count), :], out_ref.at[:, at, :], out_sem.at[sem])

    for g in range(groups):
        bring(g).start()

    def lay(c, first, last):
        def some(group, _):
            g = c * per_chunk + group
            bring(g).wait()
            for d in range(DEPTH):
                block = in_buf[g, d].astype(jnp.float32)
                at = pl.ds(d * PITCH, slots)
                left_ref[at, :] = jnp.transpose(block[:LANES])
                right_ref[at, pl.ds(0, b - LANES)] = jnp.transpose(block[LANES:])
            rows = pl.ds(pl.multiple_of(group * DEPTH, DEPTH), DEPTH)
            for s in range(slots):
                at = pl.ds(s, DEPTH, stride=PITCH)
                out_buf[c, s, rows, pl.ds(0, LANES)] = left_ref[at, :].astype(jnp.bfloat16)
                out_buf[c, s, rows, pl.ds(LANES, b - LANES)] = right_ref[at, :][:, : b - LANES].astype(jnp.bfloat16)
            return 0

        lax.fori_loop(first, last, some, 0)

    parts = [(c, 0, many, c) for c in range(chunks - 1)]
    parts += [(chunks - 1, 0, head, chunks - 1), (chunks - 1, head, many - head, chunks)]
    for c, start, count, sem in parts:
        lay(c, start // DEPTH, (start + count) // DEPTH)
        send(c, start, count, sem).start()
    for c, start, count, sem in parts:
        send(c, start, count, sem).wait()


def relayout(jac):
    d, b, slots = jac.shape
    many = d // CHUNKS
    scratch = pltpu.VMEM((DEPTH * PITCH, LANES), jnp.float32)
    anywhere = pl.BlockSpec(memory_space=pltpu.HBM)
    return pl.pallas_call(
        relayout_kernel,
        out_shape=pltpu.HBM((slots, d, b), jac.dtype),
        in_specs=[anywhere],
        out_specs=anywhere,
        scratch_shapes=[
            pltpu.VMEM((d // DEPTH, DEPTH, b, slots), jac.dtype),
            pltpu.VMEM((CHUNKS, slots, many, b), jac.dtype),
            scratch,
            scratch,
            pltpu.SemaphoreType.DMA((d // DEPTH,)),
            pltpu.SemaphoreType.DMA((CHUNKS + 1,)),
        ],
        compiler_params=params(40),
        name="relayout",
    )(in_hbm(jac))


def pow2(exponent):
    return jnp.exp2(exponent).astype(jnp.bfloat16).astype(jnp.float32)


def terms_kernel(
    rows_ref, count_ref, cols_ref, own_ref, other_ref, jac_ref, out_ref, jac_buf, faces_ref, left_ref, right_ref, out_buf, sem, out_sem
):
    slots, b, _ = jac_buf.shape
    k = out_buf.shape[0]
    pieces, _, per = own_ref.shape
    core = lax.axis_index("core")

    def bring(c):
        at = pl.ds(c * GROUP, GROUP)
        return pltpu.make_async_copy(jac_ref.at[at], jac_buf.at[at], sem.at[c])

    def send(i):
        return pltpu.make_async_copy(out_buf.at[i], out_ref.at[i], out_sem.at[i])

    for c in range(slots // GROUP):
        bring(c).start()
    for i in range(pieces):
        faces_ref[pl.ds(i * per, per), pl.ds(0, b)] = jnp.transpose(own_ref[i])
        faces_ref[pl.ds((pieces + i) * per, per), pl.ds(0, b)] = jnp.transpose(other_ref[i])

    def some(c, _):
        bring(c).wait()
        for j in range(GROUP):
            slot = c * GROUP + j
            row = rows_ref[slot]
            home = row // k
            owner = home & 1
            piece = (home // 2) ^ (owner * (pieces - 1))
            place = ((owner ^ core) * pieces + piece) * per + (row & (k - 1)) * k
            lhs = faces_ref[pl.ds(pl.multiple_of(place, k), k), pl.ds(0, b)]
            term = jnp.dot(lhs, jac_buf[slot], preferred_element_type=jnp.float32)
            at = pl.ds(pl.multiple_of(slot * TERM_PITCH, 4), k)
            left_ref[at, :] = term[:, :LANES]
            right_ref[at, pl.ds(0, b - LANES)] = term[:, LANES:]
        return 0

    lax.fori_loop(0, slots // GROUP, some, 0)
    meta_row = lax.broadcasted_iota(jnp.int32, (8, slots), 0)
    slot_index = lax.broadcasted_iota(jnp.int32, (1, slots), 1)
    cols = jnp.where(slot_index < count_ref[0, 0], cols_ref[...], -1).astype(jnp.float32)
    for i in range(k):
        at = pl.ds(i, slots, stride=TERM_PITCH)
        left = jnp.transpose(left_ref[at, :])
        right = jnp.transpose(right_ref[at, :])[: b - LANES]
        flipped = jnp.concatenate([left, right], axis=0)
        top = jnp.max(jnp.abs(flipped), axis=0, keepdims=True)
        exponent = jnp.ceil(jnp.log2(jnp.maximum(top, TINY)) + 0.01) - BITS
        scaled = jnp.clip(jnp.round(flipped * pow2(-exponent)), -LIMIT, LIMIT)
        meta = jnp.where(meta_row == 0, exponent, jnp.where(meta_row == 1, cols, 0.0))
        out_buf[i] = jnp.concatenate([scaled, meta], axis=0).astype(jnp.int32).astype(jnp.int16)
        send(i).start()
    for i in range(k):
        send(i).wait()


def make_terms(rows, count, cols, own, other, jac, k):
    slots, b, _ = jac.shape
    pieces, _, per = own.shape
    scratch = pltpu.VMEM((slots * TERM_PITCH, LANES), jnp.float32)
    return pl.pallas_call(
        terms_kernel,
        out_shape=pltpu.HBM((k, b + 8, slots), jnp.int16),
        in_specs=[in_smem(), in_smem(), in_vmem(), in_vmem(), in_vmem(), pl.BlockSpec(memory_space=pltpu.HBM)],
        out_specs=pl.BlockSpec(memory_space=pltpu.HBM),
        scratch_shapes=[
            pltpu.VMEM((slots, b, b), jac.dtype),
            pltpu.VMEM((2 * pieces * per, 2 * LANES), jnp.bfloat16),
            scratch,
            scratch,
            pltpu.VMEM((k, b + 8, slots), jnp.int16),
            pltpu.SemaphoreType.DMA((slots // GROUP,)),
            pltpu.SemaphoreType.DMA((k,)),
        ],
        compiler_params=params(32),
        name="terms",
    )(rows, count, cols, own, other, in_hbm(jac))


def sum_kernel(got_ref, out_ref, lhs_ref, pick_ref):
    tiles, _, slots = got_ref.shape
    b, faces = out_ref.shape
    face = lax.broadcasted_iota(jnp.int32, (faces, slots), 0)
    for t in range(tiles):
        got = got_ref[t].astype(jnp.int32)
        high = got[:b] >> 8
        low = got[:b] & 255
        scale = pow2(got[b : b + 1].astype(jnp.float32))
        pick = jnp.where(face == got[b + 1 : b + 2], scale, 0.0)
        at = pl.ds(t * slots, slots)
        pick_ref[:, at] = pick.astype(jnp.bfloat16)
        lhs_ref[0:b, at] = (high.astype(jnp.float32) * 256.0).astype(jnp.bfloat16)
        lhs_ref[b : 2 * b, at] = low.astype(jnp.float32).astype(jnp.bfloat16)
    both = lax.dot_general(
        lhs_ref[...], pick_ref[...], (((1,), (1,)), ((), ())), preferred_element_type=jnp.float32
    )
    out_ref[...] = (both[:b] + both[b:]).astype(jnp.bfloat16)


def add_up(got, faces):
    tiles, rows, slots = got.shape
    b = rows - 8
    return pl.pallas_call(
        sum_kernel,
        out_shape=pltpu.VMEM((b, faces), jnp.bfloat16),
        in_specs=[in_vmem()],
        out_specs=in_vmem(),
        scratch_shapes=[
            pltpu.VMEM((2 * b, tiles * slots), jnp.bfloat16),
            pltpu.VMEM((faces, tiles * slots), jnp.bfloat16),
        ],
        compiler_params=params(),
        name="add_up",
    )(got)


def both_ways(groups):
    return [[2 * i for i in groups], [2 * i + 1 for i in reversed(groups)]]


def gather_result(mine):
    xlo = lax.axis_index("xlo")
    z = lax.axis_index("z")
    core = lax.axis_index("core")

    def shift(turn, cross):
        steps = (turn, -turn)
        return [
            (x * 16 + i * 2 + c, (x ^ cross) * 16 + (i + steps[c]) % 8 * 2 + c)
            for x in range(2)
            for i in range(8)
            for c in range(2)
        ]

    def send(piece, turn, cross):
        return lax.ppermute(piece, ("xlo", "z", "core"), shift(turn, cross))

    def up(piece):
        return send(piece, 1, 0)

    def down(piece):
        return send(piece, -1, 0)

    def across(piece):
        return send(piece, 0, 1)

    def both(one, two):
        return jnp.stack([one, two])

    held = {(0, 0): mine}
    held[0, -1], held[0, 1] = up(mine), down(mine)
    held[1, 0] = across(mine)
    held[0, -2], held[0, 2] = up(held[0, -1]), down(held[0, 1])
    held[1, -1], held[1, 1] = across(both(held[0, -1], held[0, 1]))
    held[0, -3], held[0, 3] = up(held[0, -2]), down(held[0, 2])
    held[1, -2], held[1, 2] = across(both(held[0, -2], held[0, 2]))
    held[1, -3], held[1, 3] = across(both(held[0, -3], held[0, 3]))
    held[0, 4] = down(held[0, 3])
    held[1, -4] = send(held[0, -3], 1, 1)
    out = jnp.zeros((2, 8) + mine.shape, mine.dtype)
    for (x, d), piece in held.items():
        at = (z + (1 - 2 * core) * d + 8) % 8
        out = lax.dynamic_update_slice(out, piece[None, None], (xlo ^ x ^ core, at ^ (7 * core), 0, 0))
    return out


def on_device(adjoints, jac_blocks, jac_rows, jac_cols, tile_count):
    faces_here, k, b = adjoints.shape
    slots = jac_rows.shape[2]
    copies = flip(adjoints.reshape(faces_here * k, b), 8)
    own = lax.all_to_all(copies, COL, 0, 0, axis_index_groups=both_ways(range(8)))
    other = lax.ppermute(own, "core", [(0, 1), (1, 0)])
    jac = relayout(jnp.transpose(jac_blocks[0, 0], (1, 2, 0)))
    terms = make_terms(jac_rows.reshape(slots), tile_count, jac_cols.reshape(1, slots), own, other, jac, k)
    got = lax.all_to_all(terms, ROW + ("core",), 0, 0, axis_index_groups=both_ways(range(16)))
    mine = add_up(got, faces_here * 16)
    out = gather_result(mine).reshape(k, b, faces_here * 16)
    return jnp.transpose(out, (2, 0, 1))


def solution(mesh):
    parts = Mesh(mesh.devices.reshape(SIZES), AXES)
    placed = (
        P(AXES, None, None),
        P(ROW, COL, None, None, None),
        P(ROW, COL, None),
        P(ROW, COL, None),
        P(ROW, COL),
    )
    return jax.shard_map(
        on_device, mesh=parts, in_specs=placed, out_specs=P(COL, None, None), check_vma=False
    )
```

```python
import jax
import jax.numpy as jnp
from jax import lax
from jax.experimental import pallas as pl
from jax.experimental.pallas import tpu as pltpu
from jax.sharding import Mesh, PartitionSpec as P


AXES = ("xlo", "z", "xhi", "y", "core")
SIZES = (2, 8, 2, 4, 2)
ROW = ("xlo", "z")
COL = ("xhi", "y", "core")

LANES = 128
DEPTH = 8
CHUNKS = 5
PITCH = 132
TERM_PITCH = 20
GROUP = 8
BITS = 15
LIMIT = 32767.0
TINY = 1e-30


def in_vmem():
    return pl.BlockSpec(memory_space=pltpu.VMEM)


def in_smem():
    return pl.BlockSpec(memory_space=pltpu.SMEM)


def in_hbm(array):
    return pltpu.with_memory_space_constraint(array, pltpu.HBM)


def params(mib=16):
    return pltpu.CompilerParams(vmem_limit_bytes=mib << 20)


def flip_kernel(in_ref, out_ref, in_buf, out_buf, in_sem, out_sem):
    bring = pltpu.make_async_copy(in_ref, in_buf, in_sem)
    bring.start()
    bring.wait()
    out_buf[...] = jnp.transpose(in_buf[...])

    def send(i):
        return pltpu.make_async_copy(out_buf, out_ref.at[i], out_sem.at[i])

    copies = out_ref.shape[0]
    for i in range(copies):
        send(i).start()
    for i in range(copies):
        send(i).wait()


def flip(faces, copies):
    rows, b = faces.shape
    anywhere = pl.BlockSpec(memory_space=pltpu.HBM)
    return pl.pallas_call(
        flip_kernel,
        out_shape=pltpu.HBM((copies, b, rows), faces.dtype),
        in_specs=[anywhere],
        out_specs=anywhere,
        scratch_shapes=[
            pltpu.VMEM((rows, b), faces.dtype),
            pltpu.VMEM((b, rows), faces.dtype),
            pltpu.SemaphoreType.DMA,
            pltpu.SemaphoreType.DMA((copies,)),
        ],
        compiler_params=params(),
        name="flip",
    )(in_hbm(faces))


def relayout_kernel(jac_ref, out_ref, in_buf, out_buf, left_ref, right_ref, in_sem, out_sem):
    groups, _, b, slots = in_buf.shape
    chunks, _, many, _ = out_buf.shape
    per_chunk = many // DEPTH
    head = per_chunk // 2 * DEPTH

    def bring(g):
        return pltpu.make_async_copy(jac_ref.at[pl.ds(g * DEPTH, DEPTH)], in_buf.at[g], in_sem.at[g])

    def send(c, start, count, sem):
        at = pl.ds(c * many + start, count)
        return pltpu.make_async_copy(out_buf.at[c, :, pl.ds(start, count), :], out_ref.at[:, at, :], out_sem.at[sem])

    for g in range(groups):
        bring(g).start()

    def lay(c, first, last):
        def some(group, _):
            g = c * per_chunk + group
            bring(g).wait()
            for d in range(DEPTH):
                block = in_buf[g, d].astype(jnp.float32)
                at = pl.ds(d * PITCH, slots)
                left_ref[at, :] = jnp.transpose(block[:LANES])
                right_ref[at, pl.ds(0, b - LANES)] = jnp.transpose(block[LANES:])
            rows = pl.ds(pl.multiple_of(group * DEPTH, DEPTH), DEPTH)
            for s in range(slots):
                at = pl.ds(s, DEPTH, stride=PITCH)
                out_buf[c, s, rows, pl.ds(0, LANES)] = left_ref[at, :].astype(jnp.bfloat16)
                out_buf[c, s, rows, pl.ds(LANES, b - LANES)] = right_ref[at, :][:, : b - LANES].astype(jnp.bfloat16)
            return 0

        lax.fori_loop(first, last, some, 0)

    parts = [(c, 0, many, c) for c in range(chunks - 1)]
    parts += [(chunks - 1, 0, head, chunks - 1), (chunks - 1, head, many - head, chunks)]
    for c, start, count, sem in parts:
        lay(c, start // DEPTH, (start + count) // DEPTH)
        send(c, start, count, sem).start()
    for c, start, count, sem in parts:
        send(c, start, count, sem).wait()


def relayout(jac):
    d, b, slots = jac.shape
    many = d // CHUNKS
    scratch = pltpu.VMEM((DEPTH * PITCH, LANES), jnp.float32)
    anywhere = pl.BlockSpec(memory_space=pltpu.HBM)
    return pl.pallas_call(
        relayout_kernel,
        out_shape=pltpu.HBM((slots, d, b), jac.dtype),
        in_specs=[anywhere],
        out_specs=anywhere,
        scratch_shapes=[
            pltpu.VMEM((d // DEPTH, DEPTH, b, slots), jac.dtype),
            pltpu.VMEM((CHUNKS, slots, many, b), jac.dtype),
            scratch,
            scratch,
            pltpu.SemaphoreType.DMA((d // DEPTH,)),
            pltpu.SemaphoreType.DMA((CHUNKS + 1,)),
        ],
        compiler_params=params(40),
        name="relayout",
    )(in_hbm(jac))


def pow2(exponent):
    return jnp.exp2(exponent).astype(jnp.bfloat16).astype(jnp.float32)


def terms_kernel(
    rows_ref, count_ref, cols_ref, own_ref, other_ref, jac_ref, out_ref, jac_buf, faces_ref, left_ref, right_ref, out_buf, sem, out_sem
):
    slots, b, _ = jac_buf.shape
    k = out_buf.shape[0]
    pieces, _, per = own_ref.shape
    core = lax.axis_index("core")

    def bring(c):
        at = pl.ds(c * GROUP, GROUP)
        return pltpu.make_async_copy(jac_ref.at[at], jac_buf.at[at], sem.at[c])

    def send(i):
        return pltpu.make_async_copy(out_buf.at[i], out_ref.at[i], out_sem.at[i])

    groups = slots // GROUP
    live = jnp.minimum((count_ref[0, 0] + GROUP - 1) // GROUP, groups)

    def fetch(c, _):
        bring(c).start()
        return 0

    lax.fori_loop(0, live, fetch, 0)
    for i in range(pieces):
        faces_ref[pl.ds(i * per, per), pl.ds(0, b)] = jnp.transpose(own_ref[i])
        faces_ref[pl.ds((pieces + i) * per, per), pl.ds(0, b)] = jnp.transpose(other_ref[i])

    def some(c, _):
        bring(c).wait()
        for j in range(GROUP):
            slot = c * GROUP + j
            row = rows_ref[slot]
            home = row // k
            owner = home & 1
            piece = (home // 2) ^ (owner * (pieces - 1))
            place = ((owner ^ core) * pieces + piece) * per + (row & (k - 1)) * k
            lhs = faces_ref[pl.ds(pl.multiple_of(place, k), k), pl.ds(0, b)]
            term = jnp.dot(lhs, jac_buf[slot], preferred_element_type=jnp.float32)
            at = pl.ds(pl.multiple_of(slot * TERM_PITCH, 4), k)
            left_ref[at, :] = term[:, :LANES]
            right_ref[at, pl.ds(0, b - LANES)] = term[:, LANES:]
        return 0

    def clear(c, _):
        height = GROUP * TERM_PITCH
        at = pl.ds(pl.multiple_of(c * height, 8), height)
        left_ref[at, :] = jnp.zeros((height, LANES), jnp.float32)
        right_ref[at, :] = jnp.zeros((height, LANES), jnp.float32)
        return 0

    lax.fori_loop(0, live, some, 0)
    lax.fori_loop(live, groups, clear, 0)
    meta_row = lax.broadcasted_iota(jnp.int32, (8, slots), 0)
    slot_index = lax.broadcasted_iota(jnp.int32, (1, slots), 1)
    cols = jnp.where(slot_index < count_ref[0, 0], cols_ref[...], -1).astype(jnp.float32)
    for i in range(k):
        at = pl.ds(i, slots, stride=TERM_PITCH)
        left = jnp.transpose(left_ref[at, :])
        right = jnp.transpose(right_ref[at, :])[: b - LANES]
        flipped = jnp.concatenate([left, right], axis=0)
        top = jnp.max(jnp.abs(flipped), axis=0, keepdims=True)
        exponent = jnp.ceil(jnp.log2(jnp.maximum(top, TINY)) + 0.01) - BITS
        scaled = jnp.clip(jnp.round(flipped * pow2(-exponent)), -LIMIT, LIMIT)
        meta = jnp.where(meta_row == 0, exponent, jnp.where(meta_row == 1, cols, 0.0))
        out_buf[i] = jnp.concatenate([scaled, meta], axis=0).astype(jnp.int32).astype(jnp.int16)
        send(i).start()
    for i in range(k):
        send(i).wait()


def make_terms(rows, count, cols, own, other, jac, k):
    slots, b, _ = jac.shape
    pieces, _, per = own.shape
    scratch = pltpu.VMEM((slots * TERM_PITCH, LANES), jnp.float32)
    return pl.pallas_call(
        terms_kernel,
        out_shape=pltpu.HBM((k, b + 8, slots), jnp.int16),
        in_specs=[in_smem(), in_smem(), in_vmem(), in_vmem(), in_vmem(), pl.BlockSpec(memory_space=pltpu.HBM)],
        out_specs=pl.BlockSpec(memory_space=pltpu.HBM),
        scratch_shapes=[
            pltpu.VMEM((slots, b, b), jac.dtype),
            pltpu.VMEM((2 * pieces * per, 2 * LANES), jnp.bfloat16),
            scratch,
            scratch,
            pltpu.VMEM((k, b + 8, slots), jnp.int16),
            pltpu.SemaphoreType.DMA((slots // GROUP,)),
            pltpu.SemaphoreType.DMA((k,)),
        ],
        compiler_params=params(32),
        name="terms",
    )(rows, count, cols, own, other, in_hbm(jac))


def sum_kernel(got_ref, out_ref, lhs_ref, pick_ref):
    tiles, _, slots = got_ref.shape
    b, faces = out_ref.shape
    face = lax.broadcasted_iota(jnp.int32, (faces, slots), 0)
    for t in range(tiles):
        got = got_ref[t].astype(jnp.int32)
        high = got[:b] >> 8
        low = got[:b] & 255
        scale = pow2(got[b : b + 1].astype(jnp.float32))
        pick = jnp.where(face == got[b + 1 : b + 2], scale, 0.0)
        at = pl.ds(t * slots, slots)
        pick_ref[:, at] = pick.astype(jnp.bfloat16)
        lhs_ref[0:b, at] = (high.astype(jnp.float32) * 256.0).astype(jnp.bfloat16)
        lhs_ref[b : 2 * b, at] = low.astype(jnp.float32).astype(jnp.bfloat16)
    both = lax.dot_general(
        lhs_ref[...], pick_ref[...], (((1,), (1,)), ((), ())), preferred_element_type=jnp.float32
    )
    out_ref[...] = (both[:b] + both[b:]).astype(jnp.bfloat16)


def add_up(got, faces):
    tiles, rows, slots = got.shape
    b = rows - 8
    return pl.pallas_call(
        sum_kernel,
        out_shape=pltpu.VMEM((b, faces), jnp.bfloat16),
        in_specs=[in_vmem()],
        out_specs=in_vmem(),
        scratch_shapes=[
            pltpu.VMEM((2 * b, tiles * slots), jnp.bfloat16),
            pltpu.VMEM((faces, tiles * slots), jnp.bfloat16),
        ],
        compiler_params=params(),
        name="add_up",
    )(got)


def both_ways(groups):
    return [[2 * i for i in groups], [2 * i + 1 for i in reversed(groups)]]


def gather_result(mine):
    xlo = lax.axis_index("xlo")
    z = lax.axis_index("z")
    core = lax.axis_index("core")

    def shift(turn, cross):
        steps = (turn, -turn)
        return [
            (x * 16 + i * 2 + c, (x ^ cross) * 16 + (i + steps[c]) % 8 * 2 + c)
            for x in range(2)
            for i in range(8)
            for c in range(2)
        ]

    def send(piece, turn, cross):
        return lax.ppermute(piece, ("xlo", "z", "core"), shift(turn, cross))

    def up(piece):
        return send(piece, 1, 0)

    def down(piece):
        return send(piece, -1, 0)

    def across(piece):
        return send(piece, 0, 1)

    def both(one, two):
        return jnp.stack([one, two])

    held = {(0, 0): mine}
    held[0, -1], held[0, 1] = up(mine), down(mine)
    held[1, 0] = across(mine)
    held[0, -2], held[0, 2] = up(held[0, -1]), down(held[0, 1])
    held[1, -1], held[1, 1] = across(both(held[0, -1], held[0, 1]))
    held[0, -3], held[0, 3] = up(held[0, -2]), down(held[0, 2])
    held[1, -2], held[1, 2] = across(both(held[0, -2], held[0, 2]))
    held[1, -3], held[1, 3] = across(both(held[0, -3], held[0, 3]))
    held[0, 4] = down(held[0, 3])
    held[1, -4] = send(held[0, -3], 1, 1)
    out = jnp.zeros((2, 8) + mine.shape, mine.dtype)
    for (x, d), piece in held.items():
        at = (z + (1 - 2 * core) * d + 8) % 8
        out = lax.dynamic_update_slice(out, piece[None, None], (xlo ^ x ^ core, at ^ (7 * core), 0, 0))
    return out


def on_device(adjoints, jac_blocks, jac_rows, jac_cols, tile_count):
    faces_here, k, b = adjoints.shape
    slots = jac_rows.shape[2]
    copies = flip(adjoints.reshape(faces_here * k, b), 8)
    own = lax.all_to_all(copies, COL, 0, 0, axis_index_groups=both_ways(range(8)))
    other = lax.ppermute(own, "core", [(0, 1), (1, 0)])
    jac = relayout(jnp.transpose(jac_blocks[0, 0], (1, 2, 0)))
    terms = make_terms(jac_rows.reshape(slots), tile_count, jac_cols.reshape(1, slots), own, other, jac, k)
    got = lax.all_to_all(terms, ROW + ("core",), 0, 0, axis_index_groups=both_ways(range(16)))
    mine = add_up(got, faces_here * 16)
    out = gather_result(mine).reshape(k, b, faces_here * 16)
    return jnp.transpose(out, (2, 0, 1))


def solution(mesh):
    parts = Mesh(mesh.devices.reshape(SIZES), AXES)
    placed = (
        P(AXES, None, None),
        P(ROW, COL, None, None, None),
        P(ROW, COL, None),
        P(ROW, COL, None),
        P(ROW, COL),
    )
    return jax.shard_map(
        on_device, mesh=parts, in_specs=placed, out_specs=P(COL, None, None), check_vma=False
    )
```
